256 devices in a mesh: dp: 8 (over y, core), label: 32 (over x, z).
Axes of the slice: x: 4, y: 4, z: 8, core: 2. Of those that a mesh axis runs over, the one named last changes fastest.
Arguments:
- queries: bfloat16 [32768, 512], P(('dp', 'label')), may hold values from -200 to 200
- shortlist: int32 [32768, 4], P(('dp', 'label')), may hold values from 0 to 511, all different within a row; in each aligned block of 128 rows (0 to 127, 128 to 255, ...) at most 2 rows name the same one
- slab_slot: int32 [512], replicated, may hold values from 0 to 511, each once
- top_target: int32 [32768], P(('dp', 'label')), may hold values from 0 to 2047
- leaf_target: int32 [32768], P(('dp', 'label')), may hold values from 0 to 127
- top_weight: bfloat16 [2048, 512], P('label'), may hold values from -0.25 to 0.25
- mid_weight: bfloat16 [512, 512], P(('dp', 'label')), may hold values from -0.25 to 0.25
- leaf_weight: bfloat16 [512, 128, 512], P(('dp', 'label')), may hold values from -0.25 to 0.25
Outputs:
- query_grad: float32 [32768, 512], P(('dp', 'label'))
- top_grad: float32 [2048, 512], P('label')
- mid_grad: float32 [512, 512], P(('dp', 'label'))
- leaf_grad: float32 [512, 128, 512], P(('dp', 'label'))
- losses: float32 [3, 32768], P(None, ('dp', 'label'))
The draws below stay inside these ranges and needn't reach their ends.
Inputs may be any that keep to these rules, and one draw needn't show every extreme that they name: `shortlist`: each query names 4 different mid clusters; among the 128 queries of one device no cluster is named more than 2 times. Each cluster's mid and leaf rows are row slab_slot[c] of mid_weight and leaf_weight; every row is used once.
All inputs are finite; a program needn't handle non-finite values.
Results may differ from the reference program's by a relative error of at most 0.003.
Values may be sent and summed in bfloat16 or wider, within the bound.
A program may use at most 64 MiB of HBM per device.

```python
import math
import jax
import jax.numpy as jnp
import numpy as np
from jax import lax

D = 512
TOPC = 2048
LEAF = 128
SHORT = 4
BLOCKS = 512
QD = 128
QTOT = 32768
CAPB = 2
DEVICES = 256


def draw_queries(key, part):
    values = jax.random.normal(key, (QTOT, D), jnp.float32)
    values = jnp.clip(values, -5.0, 5.0)
    return values.astype(jnp.bfloat16)


def touch_ends(drawn, own_key, smallest, largest):
    dims = drawn.shape
    place = [jax.random.randint(jax.random.fold_in(own_key, axis), (), 0, dims[axis]) for axis in range(len(dims))]
    drawn = drawn.at[tuple(place)].set(smallest)
    longest = dims.index(max(dims))
    place[longest] = (place[longest] + 1) % dims[longest]
    return drawn.at[tuple(place)].set(largest)


def block_scale(own_key, dims, cuts, low, high):
    level = 1.0
    for dim, parts in cuts:
        draws = jax.random.uniform(jax.random.fold_in(jax.random.fold_in(own_key, 6), dim), (parts,), jnp.float32, low / len(cuts), high / len(cuts))
        level = level * jnp.repeat(jnp.exp(draws), dims[dim] // parts).reshape((-1,) + (1,) * (len(dims) - 1 - dim))
    return level


def routed_block(rng, own, number, rows, count, top, most, skew):
    sequence = jax.random.permutation(rng, count)
    packed, common = portions_of(count, rows * top, most, skew, True), portions_of(count, rows * top, most, skew, False)
    places = jnp.arange(count)

    def named(tallies, rotation):
        used = int((tallies > 0).sum())
        fixed = max(1, used // 4)
        shifted = fixed + (places - fixed + rotation * (used - fixed)) % max(1, count - fixed)
        return jnp.zeros((count,), jnp.int32).at[sequence[jnp.where(places < fixed, places, shifted)]].set(jnp.asarray(tallies, jnp.int32))

    tallies = jnp.where(number % 4 == 0, named(packed, number // 4), named(common, number - number // 4 - 1))
    mixed = jax.random.permutation(jax.random.fold_in(own, 3), count)
    donor, sink = mixed[0:count // 2 * 2:2], mixed[1:count // 2 * 2:2]
    margin = jnp.minimum(tallies[donor] - 1, most - tallies[sink]) // 2
    margin = jnp.where((donor == sequence[0]) | (sink == sequence[0]) | (tallies[sink] == 0), 0, jnp.maximum(margin, 0))
    shifted = jax.random.randint(jax.random.fold_in(own, 4), (count // 2,), 0, 1 << 20) % (margin + 1)
    tallies = tallies.at[donor].add(-shifted).at[sink].add(shifted)
    items = jnp.searchsorted(jnp.cumsum(tallies), jnp.arange(rows * top), side="right").astype(jnp.int32)
    listing = items.reshape(top, rows).T
    listing = listing[jax.random.permutation(jax.random.fold_in(own, 1), rows)]
    rotation = jax.random.randint(jax.random.fold_in(own, 2), (rows, 1), 0, top)
    return jnp.take_along_axis(listing, (jnp.arange(top)[None, :] + rotation) % top, axis=1)


def portions_of(amount, total, most, skew, full):
    loads = [(1 << 20) // math.isqrt(rank ** skew) + 1 for rank in range(1, amount + 1)]
    largest = most if full else min(most, max(-(-total // amount), total * loads[0] // sum(loads)))
    least = 1 if total - largest >= amount - 1 else 0
    counts, rest = [largest] + [least] * (amount - 1), total - largest - least * (amount - 1)
    while rest > 0:
        free = [i for i in range(1, amount) if counts[i] < largest] or [i for i in range(1, amount) if counts[i] < most]
        mass, left = sum([loads[i] for i in free]), rest
        for i in free:
            addition = min(most - counts[i], max(1, left * loads[i] // mass), rest)
            counts[i] = counts[i] + addition
            rest = rest - addition
    return np.array(counts)


def normal_values(key, dims, scale, bound, cuts=(), kind=jnp.bfloat16):
    level = block_scale(key, dims, cuts, -0.22, 0.18) if cuts else 1.0
    values = jax.random.normal(key, dims, jnp.float32) * scale * level
    return jnp.minimum(jnp.maximum(values, -bound), bound).astype(kind)


def setup_inputs(seed: int = 0) -> dict:
    splits = jax.random.split(jax.random.key(seed), 9)
    queries = draw_queries(jax.random.fold_in(splits[8], 71), 0)
    shortlist_keys = jax.random.split(jax.random.fold_in(splits[1], 1), QTOT // QD)
    shortlist_turns = jax.random.permutation(jax.random.fold_in(splits[1], 3), QTOT // QD)
    shortlist = jax.vmap(lambda own, number: routed_block(jax.random.fold_in(splits[1], 2), own, number, QD, BLOCKS, SHORT, CAPB, 2))(shortlist_keys, shortlist_turns).reshape((QTOT, SHORT))
    slab_slot = jax.random.permutation(splits[2], BLOCKS).astype(jnp.int32)
    top_target = touch_ends(jax.random.randint(splits[3], (QTOT,), 0, TOPC), jax.random.fold_in(splits[3], 1), 0, TOPC - 1).astype(jnp.int32)
    leaf_target = touch_ends(jax.random.randint(splits[4], (QTOT,), 0, LEAF), jax.random.fold_in(splits[4], 1), 0, LEAF - 1).astype(jnp.int32)
    top_weight = normal_values(splits[5], (TOPC, D), D ** -0.5, 0.25, ((0, 32),))
    mid_weight = normal_values(splits[6], (BLOCKS, D), D ** -0.5, 0.25, ((0, 256),))
    leaf_weight = normal_values(splits[7], (BLOCKS, LEAF, D), D ** -0.5, 0.25, ((0, 256),))
    return dict(queries=queries, shortlist=shortlist, slab_slot=slab_slot, top_target=top_target, leaf_target=leaf_target, top_weight=top_weight, mid_weight=mid_weight, leaf_weight=leaf_weight)


def top_level(queries, top_target, top_weight):
    step_rows = QD * 8
    steps_count = queries.shape[0] // step_rows
    query_blocks = queries.reshape(steps_count, step_rows, D)
    target_blocks = top_target.reshape(steps_count, step_rows)
    columns = jnp.arange(TOPC, dtype=jnp.int32)

    def visit_block(accumulator, pieces):
        row_block, targets = pieces
        scores = jnp.dot(row_block, top_weight.T, preferred_element_type=jnp.float32)
        totals = jax.nn.logsumexp(scores, axis=1)
        target_hit = targets[:, None] == columns[None, :]
        top_loss = totals - jnp.sum(jnp.where(target_hit, scores, jnp.zeros_like(scores)), axis=1)
        dscore = (jnp.exp(scores - totals[:, None]) - target_hit.astype(jnp.float32)).astype(jnp.bfloat16)
        accumulator = accumulator + jnp.dot(dscore.T, row_block, preferred_element_type=jnp.float32)
        top_back = jnp.dot(dscore, top_weight, preferred_element_type=jnp.float32)
        return accumulator, (top_loss, top_back)

    start_grad = jnp.zeros((TOPC, D), jnp.float32)
    top_grad, (top_loss, top_back) = lax.scan(visit_block, start_grad, (query_blocks, target_blocks))
    return top_grad, top_loss.reshape(-1), top_back.reshape(-1, D)


def build_table(shortlist, slab_slot):
    position = slab_slot[shortlist].reshape(-1).astype(jnp.int32)
    sort_order = jnp.argsort(position, stable=True).astype(jnp.int32)
    ranked = position[sort_order]
    run_start = jnp.searchsorted(ranked, ranked, side="left").astype(jnp.int32)
    slot_rank = jnp.arange(ranked.shape[0], dtype=jnp.int32) - run_start
    pair_table = jnp.full((BLOCKS, DEVICES * CAPB), QTOT * SHORT, jnp.int32)
    return pair_table.at[ranked, slot_rank].set(sort_order)


def group_inputs(queries, pair_table, mid_weight, leaf_weight, group_index):
    padded = jnp.concatenate([queries, jnp.zeros((1, D), queries.dtype)], axis=0)
    group_table = lax.dynamic_slice_in_dim(pair_table, group_index * 16, 16, 0)
    query_index = (group_table // SHORT).astype(jnp.int32)
    row_block = padded[query_index].astype(jnp.float32)
    leaf_rows = lax.dynamic_slice_in_dim(leaf_weight, group_index * 16, 16, 0).astype(jnp.float32)
    mid_rows = lax.dynamic_slice_in_dim(mid_weight, group_index * 16, 16, 0).astype(jnp.float32)
    return group_table, query_index, row_block, leaf_rows, mid_rows


def leaf_forward(queries, pair_table, pair_codes, mid_weight, leaf_weight):
    codes_ext = jnp.concatenate([pair_codes, jnp.full((1,), -2, jnp.int32)])
    labels = jnp.arange(LEAF, dtype=jnp.int32)

    def visit_group(group_index):
        group_table, query_index, row_block, leaf_rows, mid_rows = group_inputs(queries, pair_table, mid_weight, leaf_weight, group_index)
        scores = jnp.einsum("gsd,gld->gsl", row_block, leaf_rows)
        mid_scores = jnp.einsum("gsd,gd->gs", row_block, mid_rows)
        block_lse = jax.nn.logsumexp(scores, axis=-1)
        target_hit = codes_ext[group_table][..., None] == labels
        target = jnp.sum(jnp.where(target_hit, scores, jnp.zeros_like(scores)), axis=-1)
        return mid_scores, block_lse, target

    outputs = lax.map(visit_group, jnp.arange(BLOCKS // 16, dtype=jnp.int32))
    flat_index = pair_table.reshape(-1)
    results = []
    for values in outputs:
        placed = jnp.zeros((QTOT * SHORT + 1,), jnp.float32).at[flat_index].set(values.reshape(-1))
        results.append(placed[:-1].reshape(QTOT, SHORT))
    return results[0], results[1], results[2]


def leaf_backward(queries, pair_table, pair_codes, pair_delta, pair_lse, mid_weight, leaf_weight):
    codes_ext = jnp.concatenate([pair_codes, jnp.full((1,), -2, jnp.int32)])
    delta_ext = jnp.concatenate([pair_delta, jnp.zeros((1,), pair_delta.dtype)])
    lse_ext = jnp.concatenate([pair_lse, jnp.zeros((1,), jnp.float32)])
    labels = jnp.arange(LEAF, dtype=jnp.int32)

    def visit_group(accumulator, group_index):
        group_table, query_index, row_block, leaf_rows, mid_rows = group_inputs(queries, pair_table, mid_weight, leaf_weight, group_index)
        scores = jnp.einsum("gsd,gld->gsl", row_block, leaf_rows)
        group_codes = codes_ext[group_table]
        live_slot = group_codes >= -1
        target_hit = (group_codes[..., None] == labels).astype(jnp.float32)
        slot_lse = lse_ext[group_table]
        leaf_delta = jnp.where(live_slot[..., None], jnp.exp(scores - slot_lse[..., None]) - target_hit, jnp.zeros_like(scores)).astype(jnp.bfloat16)
        leaf_float = leaf_delta.astype(jnp.float32)
        mid_float = delta_ext[group_table].astype(jnp.float32)
        leaf_part = jnp.einsum("gsl,gsd->gld", leaf_float, row_block)
        mid_part = jnp.einsum("gs,gsd->gd", mid_float, row_block)
        pair_back = (jnp.einsum("gsl,gld->gsd", leaf_float, leaf_rows) + mid_float[..., None] * mid_rows[:, None, :]).astype(jnp.bfloat16)
        accumulator = accumulator.at[query_index.reshape(-1)].add(pair_back.reshape(-1, D).astype(jnp.float32))
        return accumulator, (mid_part, leaf_part)

    start_sum = jnp.zeros((QTOT + 1, D), jnp.float32)
    summed, (mid_grad, leaf_grad) = lax.scan(visit_group, start_sum, jnp.arange(BLOCKS // 16, dtype=jnp.int32))
    return summed[:-1], mid_grad.reshape(BLOCKS, D), leaf_grad.reshape(BLOCKS, LEAF, D)


def reference(queries, shortlist, slab_slot, top_target, leaf_target, top_weight, mid_weight, leaf_weight):
    top_grad, top_loss, top_back = top_level(queries, top_target, top_weight)
    pair_table = build_table(shortlist, slab_slot)
    first_slot = (jnp.arange(SHORT, dtype=jnp.int32) == 0)[None, :]
    pair_codes = jnp.where(first_slot, leaf_target[:, None], -1).astype(jnp.int32).reshape(-1)
    mid_scores, block_lse, target = leaf_forward(queries, pair_table, pair_codes, mid_weight, leaf_weight)
    mid_totals = jax.nn.logsumexp(mid_scores, axis=1)
    mid_loss = mid_totals - mid_scores[:, 0]
    mid_delta = (jnp.exp(mid_scores - mid_totals[:, None]) - first_slot.astype(jnp.float32)).astype(jnp.bfloat16)
    leaf_lse = jax.nn.logsumexp(block_lse, axis=1)
    leaf_loss = leaf_lse - target[:, 0]
    pair_lse = jnp.broadcast_to(leaf_lse[:, None], (QTOT, SHORT)).reshape(-1)
    summed, mid_grad, leaf_grad = leaf_backward(queries, pair_table, pair_codes, mid_delta.reshape(-1), pair_lse, mid_weight, leaf_weight)
    query_grad = top_back + summed
    losses = jnp.stack([top_loss, mid_loss, leaf_loss])
    return query_grad, top_grad, mid_grad, leaf_grad, losses
```

```python
import jax
import jax.numpy as jnp
from jax import lax
from jax.experimental import pallas as pl
from jax.experimental.pallas import tpu as pltpu
from jax.sharding import PartitionSpec as P

D = 512
BLOCKS = 512
QD = 128
SHORT = 4
LEAF = 128
NZ = 8
NX = 4
NDP = 8
PLANE = NX * NDP
ROWS = 16
SLOTS = PLANE * ROWS
TABLE = 16
BLK = QD + TABLE
ORDER = (0, 1, 7, 2, 6, 3, 5, 4)
IDX = tuple(ORDER.index(o) for o in range(NZ))
NEG = -1e30
MESH = pl.DeviceIdType.MESH
F32 = jnp.float32
BF16 = jnp.bfloat16
NT = (((1,), (1,)), ((), ()))
TN = (((0,), (0,)), ((), ()))
NN = (((1,), (0,)), ((), ()))


def dot(a, b, dims):
    return lax.dot_general(a, b, dims, preferred_element_type=F32)


def split3(v):
    hi = v.astype(BF16)
    rest = v - hi.astype(F32)
    mid = rest.astype(BF16)
    low = (rest - mid.astype(F32)).astype(BF16)
    return hi, mid, low


def iota(shape, dim):
    return lax.broadcasted_iota(jnp.int32, shape, dim)


def kernel(
    blk_ref, leaf_ref, mid_ref, topw_ref,
    qg_ref, tg_ref, mg_ref, lg_ref, loss_ref,
    gq, xw, wext, oht, pk, rb, sk, ts, live_ref, info, cmsg, crecv, emsg, erecv, fmsg, frecv,
    stat, zstat, zlse, part, ob, pbk, tgs, tgr, losss, lossr, rsS, rsR,
    psend, precv, agsend, agrecv, rssend, rsrecv, zsend, zrecv, wsend, wrecv, osend, orecv,
):
    dp = lax.axis_index("dp")
    label = lax.axis_index("label")
    x = label // NZ
    z = label % NZ
    me = x * NDP + dp

    def plane_id(t):
        return (t % NDP, (t // NDP) * NZ + z)

    def z_id(d):
        return (dp, x * NZ + (z + d) % NZ)

    def x_id(d):
        return (dp, ((x + d) % NX) * NZ + z)

    def dp_id(d):
        return ((dp + d) % NDP, label)

    gq[0] = blk_ref[...]
    wext[0:256, :] = leaf_ref[...].reshape(256, D)
    wext[256:272, :] = jnp.concatenate(
        [mid_ref[...].astype(F32), jnp.zeros((14, D), F32)], axis=0
    ).astype(BF16)

    barrier = pltpu.get_barrier_semaphore()

    def greet(i, _):
        pl.semaphore_signal(barrier, inc=1, device_id=plane_id((me + i) % PLANE), device_id_type=MESH)
        return 0

    lax.fori_loop(1, PLANE, greet, 0)
    for d in range(1, NZ):
        pl.semaphore_signal(barrier, inc=1, device_id=z_id(d), device_id_type=MESH)
    pl.semaphore_wait(barrier, PLANE - 1 + NZ - 1)

    cuts = ((0, 80), (80, 64))

    def ag(direction, hop, chunk):
        start, length = cuts[chunk]
        if direction == 0:
            src, dst, to = IDX[(NZ - hop + 1) % NZ], IDX[NZ - hop], 1
        else:
            src, dst, to = IDX[hop - 1], IDX[hop], NZ - 1
        rows = pl.ds(start, length)
        return pltpu.make_async_remote_copy(
            src_ref=gq.at[src, rows], dst_ref=gq.at[dst, rows],
            send_sem=agsend.at[direction, hop - 1, chunk],
            recv_sem=agrecv.at[direction, hop - 1, chunk],
            device_id=z_id(to), device_id_type=MESH,
        )

    def flows(hop):
        return [(0, 0), (1, 1), (1, 0), (0, 1)] if hop < 4 else [(0, 0), (1, 1)]

    for direction, chunk in flows(1):
        ag(direction, 1, chunk).start()

    def wcopy(d):
        return pltpu.make_async_remote_copy(
            src_ref=topw_ref, dst_ref=xw.at[x], send_sem=wsend.at[d], recv_sem=wrecv.at[d],
            device_id=x_id(d), device_id_type=MESH,
        )

    def wwait(d):
        return pltpu.make_async_remote_copy(
            src_ref=topw_ref, dst_ref=xw.at[(x - d + NX) % NX], send_sem=wsend.at[d],
            recv_sem=wrecv.at[d], device_id=x_id(d), device_id_type=MESH,
        )

    for d in range(1, NX):
        wcopy(d).start()
    xw[x] = topw_ref[...]

    def plane_send(phase, source, target):
        def body(i, _):
            t = (me + i) % PLANE
            pltpu.make_async_remote_copy(
                src_ref=source(t), dst_ref=target(me), send_sem=psend.at[phase, i],
                recv_sem=precv.at[phase, i], device_id=plane_id(t), device_id_type=MESH,
            ).start()
            return 0

        lax.fori_loop(1, PLANE, body, 0)

    def plane_wait(phase, source, target, sent):
        def body(i, _):
            t = (me + i) % PLANE
            f = (me - i + PLANE) % PLANE
            copy = pltpu.make_async_remote_copy(
                src_ref=source(t), dst_ref=target(f), send_sem=psend.at[phase, i],
                recv_sem=precv.at[phase, i], device_id=plane_id(t), device_id_type=MESH,
            )
            if sent:
                copy.wait_send()
            else:
                copy.wait_recv()
            return 0

        lax.fori_loop(1, PLANE, body, 0)

    exchanges = {
        "rows0": (0, lambda t: pk.at[0, t], lambda f: rb.at[0, f]),
        "rows1": (1, lambda t: pk.at[1, t], lambda f: rb.at[1, f]),
        "code": (2, lambda t: cmsg.at[t // NDP], lambda f: crecv.at[f]),
        "ex1": (3, lambda t: emsg.at[t // NDP], lambda f: erecv.at[f]),
        "ex2": (4, lambda t: fmsg.at[t // NDP], lambda f: frecv.at[f]),
        "ret1": (5, lambda t: ob.at[1, t], lambda f: pbk.at[1, f]),
        "ret0": (6, lambda t: ob.at[0, t], lambda f: pbk.at[0, f]),
        "tg": (7, lambda t: tgs.at[t], lambda f: tgr.at[f]),
    }

    def send(name):
        plane_send(*exchanges[name])

    def arrived(name):
        plane_wait(*exchanges[name], False)

    def left(name):
        plane_wait(*exchanges[name], True)

    lane = iota((8, 128), 1)

    def regroup(received):
        groups = []
        for g in range(NX):
            out = jnp.zeros((8, 128), F32)
            for j in range(NDP):
                turned = pltpu.roll(received[g * NDP + j], ((j - dp + NDP) % NDP) * ROWS, axis=1)
                out = jnp.where(lane // ROWS == j, turned, out)
            groups.append(out)
        return jnp.concatenate(groups, axis=1)

    qid = iota((SLOTS, SLOTS), 0)

    def pack(s):
        ids = jnp.zeros((1, SLOTS), F32)
        first = jnp.zeros((1, SLOTS), F32)
        targets = []
        for o4 in range(4):
            table = gq[4 * s + o4, QD:BLK, :].astype(F32)
            row = jnp.sum(jnp.where(iota((TABLE, D), 0) == z, table, 0.0), axis=0, keepdims=True)
            ids = ids + jnp.where(row != 0.0, jnp.abs(row) + o4 * QD, 0.0)
            first = first + jnp.where(row < 0.0, 1.0, 0.0)
            targets.append(table[8:9, 0:QD])
            top = (table[8:9, QD : 2 * QD] * 16.0 + table[8:9, 2 * QD : 3 * QD]).astype(jnp.int32)
            here = ((top >> 6) & 7) == z
            place = ((top >> 9) << 6) + (top & 63)
            info[4 * s + o4 : 4 * s + o4 + 1, :] = jnp.where(here, place, -1)
        hot = jnp.where(qid == ids.astype(jnp.int32) - 1, 1.0, 0.0).astype(BF16)
        oht[s] = hot
        queries = gq[4 * s : 4 * s + 4, 0:QD, :].reshape(SLOTS, D)
        pk[s] = dot(hot, queries, TN).astype(BF16).reshape(PLANE, ROWS, D)
        wanted = jnp.broadcast_to(jnp.concatenate(targets, axis=1), (8, SLOTS)).astype(BF16)
        code = dot(wanted, hot, NN)[0:1, :]
        code = jnp.where(ids > 0.0, jnp.where(first > 0.0, code, -1.0), -2.0)
        live_ref[s : s + 1, :] = jnp.where(first > 0.0, 1.0, 0.0)
        for g in range(NX):
            cmsg[g, s : s + 1, :] = code[:, g * 128 : (g + 1) * 128]

    def top_scores(s):
        queries = gq[4 * s : 4 * s + 4, 0:QD, :].reshape(SLOTS, D)
        scores = dot(xw[...].reshape(256, D), queries, NT)
        ts[s] = scores
        largest = jnp.max(scores, axis=0, keepdims=True)
        total = largest + jnp.log(jnp.sum(jnp.exp(scores - largest), axis=0, keepdims=True))
        for o4 in range(4):
            o = ORDER[4 * s + o4]
            stat[2, o : o + 1, :] = total[:, o4 * 128 : (o4 + 1) * 128]

    def own_rows(s):
        rb[s, me] = pk[s, me]

    for hop in (2, 3):
        for direction, chunk in flows(hop):
            ag(direction, hop - 1, chunk).wait_recv()
            ag(direction, hop, chunk).start()
    pack(0)
    send("rows0")
    own_rows(0)
    for direction, chunk in flows(4):
        ag(direction, 3, chunk).wait_recv()
        ag(direction, 4, chunk).start()
    for d in range(1, NX):
        wwait(d).wait_recv()
    top_scores(0)
    for direction, chunk in ((1, 0), (0, 1)):
        ag(direction, 3, chunk).wait_recv()
    for direction, chunk in flows(4):
        ag(direction, 4, chunk).wait_recv()
    for g in range(NX):
        cmsg[g, 2:8, :] = jnp.zeros((6, 128), F32)
    pack(1)
    send("rows1")
    send("code")
    own_rows(1)
    crecv[me] = cmsg[x]
    top_scores(1)

    odd = (iota((1, SLOTS), 1) >> 3) & 1

    def holder_scores(s):
        scores = dot(wext[...], rb[s].reshape(SLOTS, D), NT)
        sk[s, 0:LEAF, :] = jnp.where(odd == 0, scores[0:LEAF], scores[LEAF : 2 * LEAF])
        sk[s, LEAF : LEAF + 8, :] = jnp.broadcast_to(
            jnp.where(odd == 0, scores[256:257], scores[257:258]), (8, SLOTS)
        )

    arrived("rows0")
    holder_scores(0)
    arrived("rows1")
    holder_scores(1)
    arrived("code")
    codes = regroup(crecv)
    label_row = iota((LEAF, SLOTS), 0)
    for s in range(2):
        chosen = sk[s, 0:LEAF, :]
        code = codes[s : s + 1, :].astype(jnp.int32)
        largest = jnp.max(chosen, axis=0, keepdims=True)
        total = largest + jnp.log(jnp.sum(jnp.exp(chosen - largest), axis=0, keepdims=True))
        target = jnp.sum(jnp.where(label_row == code, chosen, 0.0), axis=0, keepdims=True)
        middle = sk[s, LEAF : LEAF + 1, :]
        for g in range(NX):
            span = slice(g * 128, (g + 1) * 128)
            emsg[g, 4 * s : 4 * s + 1, :] = total[:, span]
            emsg[g, 4 * s + 1 : 4 * s + 2, :] = middle[:, span]
            emsg[g, 4 * s + 2 : 4 * s + 3, :] = target[:, span]
            emsg[g, 4 * s + 3 : 4 * s + 4, :] = target[:, span]
    send("ex1")
    erecv[me] = emsg[x]
    arrived("ex1")
    pairs = regroup(erecv)

    eye = iota((QD, QD), 0) == iota((QD, QD), 1)
    for s in range(2):
        hot = oht[s].astype(F32) > 0.5
        for which in range(2):
            values = jnp.where(hot, pairs[4 * s + which : 4 * s + which + 1, :], NEG)
            largest = jnp.max(values, axis=1, keepdims=True)
            total = largest + jnp.log(jnp.sum(jnp.exp(values - largest), axis=1, keepdims=True))
            for o4 in range(4):
                o = ORDER[4 * s + o4]
                piece = jnp.where(eye, total[o4 * QD : (o4 + 1) * QD], 0.0)
                stat[which, o : o + 1, :] = jnp.sum(piece, axis=0, keepdims=True)

    def zcopy(d):
        return pltpu.make_async_remote_copy(
            src_ref=stat, dst_ref=zstat.at[d], send_sem=zsend.at[0, d], recv_sem=zrecv.at[0, d],
            device_id=z_id(d), device_id_type=MESH,
        )

    for d in range(1, NZ):
        zcopy(d).start()
    for d in range(1, NZ):
        zcopy(d).wait_recv()
    for which in range(3):
        views = [stat[which]]
        for d in range(1, NZ):
            views.append(pltpu.roll(zstat[d, which], NZ - d, axis=0))
        largest = views[0]
        for view in views[1:]:
            largest = jnp.maximum(largest, view)
        total = jnp.zeros((NZ, 128), F32)
        for view in views:
            total = total + jnp.exp(view - largest)
        zlse[which] = largest + jnp.log(total)

    def query_row(which, s):
        return jnp.concatenate([zlse[which, ORDER[4 * s + o4] : ORDER[4 * s + o4] + 1, :] for o4 in range(4)], axis=1)

    slot_values = []
    for s in range(2):
        pieces = split3(query_row(0, s)) + split3(query_row(1, s))
        pieces = [piece.astype(F32) for piece in pieces] + [jnp.zeros((10, SLOTS), F32)]
        rows = dot(jnp.concatenate(pieces, axis=0).astype(BF16), oht[s], NN)
        leaf_slot = rows[0:1] + rows[1:2] + rows[2:3]
        mid_slot = rows[3:4] + rows[4:5] + rows[5:6]
        slot_values.append((leaf_slot, mid_slot))
        for g in range(NX):
            span = slice(g * 128, (g + 1) * 128)
            fmsg[g, 4 * s : 4 * s + 1, :] = leaf_slot[:, span]
            fmsg[g, 4 * s + 1 : 4 * s + 2, :] = mid_slot[:, span]
            fmsg[g, 4 * s + 2 : 4 * s + 3, :] = mid_slot[:, span]
            fmsg[g, 4 * s + 3 : 4 * s + 4, :] = mid_slot[:, span]
    send("ex2")
    frecv[me] = fmsg[x]

    weights = xw[...].reshape(256, D)
    class_row = iota((256, SLOTS), 0)
    grad = jnp.zeros((256, D), F32)
    for s in range(2):
        scores = ts[s]
        totals = query_row(2, s)
        place = jnp.concatenate([info[4 * s + o4 : 4 * s + o4 + 1, :] for o4 in range(4)], axis=1)
        hit = class_row == place
        delta = (jnp.exp(scores - totals) - jnp.where(hit, 1.0, 0.0)).astype(BF16)
        score = jnp.sum(jnp.where(hit, scores, 0.0), axis=0, keepdims=True)
        top_loss = jnp.where(place >= 0, totals - score, 0.0)
        grad = grad + dot(delta, gq[4 * s : 4 * s + 4, 0:QD, :].reshape(SLOTS, D), NN)
        part[s] = dot(delta, weights, TN)
        leaf_slot, mid_slot = slot_values[s]
        first = live_ref[s : s + 1, :] > 0.5
        leaf_loss = jnp.where(first, leaf_slot - pairs[4 * s + 2 : 4 * s + 3, :], 0.0)
        mid_loss = jnp.where(first, mid_slot - pairs[4 * s + 1 : 4 * s + 2, :], 0.0)
        pieces = split3(leaf_loss) + split3(mid_loss)
        pieces = [piece.astype(F32) for piece in pieces] + [jnp.zeros((10, SLOTS), F32)]
        rows = dot(jnp.concatenate(pieces, axis=0).astype(BF16), oht[s], NT)
        leaf_query = rows[0:1] + rows[1:2] + rows[2:3]
        mid_query = rows[3:4] + rows[4:5] + rows[5:6]
        for o4 in range(4):
            o = ORDER[4 * s + o4]
            span = slice(o4 * 128, (o4 + 1) * 128)
            losss[o] = jnp.concatenate(
                [top_loss[:, span], mid_query[:, span], leaf_query[:, span], jnp.zeros((5, 128), F32)],
                axis=0,
            )
    tgs[...] = grad.reshape(PLANE, 8, D)

    def losscopy(o):
        return pltpu.make_async_remote_copy(
            src_ref=losss.at[o], dst_ref=lossr.at[o], send_sem=zsend.at[1, o],
            recv_sem=zrecv.at[1, o], device_id=z_id(o), device_id_type=MESH,
        )

    arrived("ex2")
    scalars = regroup(frecv)
    deltas = []
    for s in (1, 0):
        code = codes[s : s + 1, :].astype(jnp.int32)
        live = code > -2
        hit = jnp.where(label_row == code, 1.0, 0.0)
        delta = jnp.where(live, jnp.exp(sk[s, 0:LEAF, :] - scalars[4 * s : 4 * s + 1, :]) - hit, 0.0)
        middle = jnp.exp(sk[s, LEAF : LEAF + 1, :] - scalars[4 * s + 1 : 4 * s + 2, :])
        middle = jnp.where(live, middle - jnp.where(code >= 0, 1.0, 0.0), 0.0)
        even = odd == 0
        whole = jnp.concatenate(
            [
                jnp.where(even, delta, 0.0), jnp.where(even, 0.0, delta),
                jnp.where(even, middle, 0.0), jnp.where(even, 0.0, middle),
                jnp.zeros((14, SLOTS), F32),
            ],
            axis=0,
        ).astype(BF16)
        deltas.append(whole)
        ob[s] = dot(whole, wext[...], TN).astype(BF16).reshape(PLANE, ROWS, D)
        send("ret1" if s else "ret0")
        pbk[s, me] = ob[s, me]
    for o in range(1, NZ):
        losscopy(o).start()
    send("tg")
    tgr[me] = tgs[me]
    grads = dot(deltas[0], rb[1].reshape(SLOTS, D), NN) + dot(deltas[1], rb[0].reshape(SLOTS, D), NN)
    lg_ref[...] = grads[0:256].reshape(2, LEAF, D)
    mg_ref[...] = grads[256:258]

    halves = (pl.ds(0, 64), pl.ds(64, 64))

    def rs(direction, hop, chunk):
        return pltpu.make_async_remote_copy(
            src_ref=rsS.at[direction, hop, halves[chunk]],
            dst_ref=rsR.at[direction, hop, halves[chunk]],
            send_sem=rssend.at[direction, hop, chunk], recv_sem=rsrecv.at[direction, hop, chunk],
            device_id=z_id(1 if direction == 0 else NZ - 1), device_id_type=MESH,
        )

    def rs_step(direction, hop, chunk):
        o = 4 - hop if direction == 0 else 4 + hop
        index = IDX[o]
        rows = pl.ds((index % 4) * QD + chunk * 64, 64)
        value = part[index // 4, rows, :]
        if hop > 1 or (hop == 1 and chunk == direction):
            rs(direction, hop - 1, chunk).wait_recv()
            value = value + rsR[direction, hop - 1, halves[chunk], :].astype(F32)
        rsS[direction, hop, halves[chunk], :] = value.astype(BF16)
        rs(direction, hop, chunk).start()

    for s in (1, 0):
        arrived("ret1" if s else "ret0")
        part[s] = part[s] + dot(oht[s], pbk[s].reshape(SLOTS, D), NN)
        if s:
            for direction in range(2):
                rs_step(direction, 0, direction)
            for direction in range(2):
                rs_step(direction, 1, 1 - direction)
            rs_step(0, 1, 0)
            rs_step(1, 1, 1)
            rs_step(1, 2, 0)
            rs_step(1, 2, 1)
    rs_step(0, 2, 1)
    rs_step(0, 2, 0)

    arrived("tg")
    tg_sum = tgr[0]
    for f in range(1, PLANE):
        tg_sum = tg_sum + tgr[f]
    tg_ref[pl.ds(pl.multiple_of(dp * 8, 8), 8), :] = tg_sum

    def tgcopy(d, who):
        rows = pl.ds(pl.multiple_of(who * 8, 8), 8)
        return pltpu.make_async_remote_copy(
            src_ref=tg_ref.at[rows], dst_ref=tg_ref.at[rows], send_sem=osend.at[d],
            recv_sem=orecv.at[d], device_id=dp_id(d), device_id_type=MESH,
        )

    for d in range(1, NDP):
        tgcopy(d, dp).start()

    for direction in range(2):
        for chunk in range(2):
            rs_step(direction, 3, chunk)

    for o in range(1, NZ):
        losscopy(o).wait_recv()
    losses = losss[0]
    for o in range(1, NZ):
        losses = losses + lossr[o]
    loss_ref[...] = losses[0:3]

    for direction in range(2):
        for chunk in range(2):
            rs(direction, 3, chunk).wait_recv()
    qg_ref[...] = part[0, 0:QD, :] + rsR[0, 3].astype(F32) + rsR[1, 3].astype(F32)

    for d in range(1, NDP):
        tgcopy(d, (dp - d + NDP) % NDP).wait_recv()

    for hop in range(1, 5):
        for direction, chunk in flows(hop):
            ag(direction, hop, chunk).wait_send()
    for d in range(1, NX):
        wcopy(d).wait_send()
    for name in exchanges:
        left(name)
    for d in range(1, NZ):
        zcopy(d).wait_send()
        losscopy(d).wait_send()
    for hop in range(4):
        for direction in range(2):
            for chunk in range(2):
                if hop > 0 or chunk == direction:
                    rs(direction, hop, chunk).wait_send()
    for d in range(1, NDP):
        tgcopy(d, dp).wait_send()


def build_block(queries, shortlist, slab_slot, top_target, leaf_target):
    z = lax.axis_index("label") % NZ
    count = QD * SHORT
    named = shortlist.reshape(-1)
    cluster = jnp.arange(BLOCKS, dtype=jnp.int32)
    position = jnp.sum(jnp.where(named[:, None] == cluster[None, :], slab_slot[None, :], 0), axis=1)
    pair = jnp.arange(count, dtype=jnp.int32)
    earlier = (position[:, None] == position[None, :]) & (pair[None, :] < pair[:, None])
    rank = jnp.sum(earlier.astype(jnp.int32), axis=1)
    k, flat = position % 2, position // 2
    holder_dp, holder_x, holder_z = flat // 32, (flat % 32) // NZ, flat % NZ
    offset = (z - holder_z + NZ) % NZ
    index = jnp.zeros_like(offset)
    for o in range(NZ):
        index = jnp.where(offset == o, IDX[o], index)
    lane = (holder_x * NDP + holder_dp) * ROWS + k * 8 + (index % 4) * 2 + rank
    query = pair // SHORT
    sign = jnp.where(pair % SHORT == 0, -1, 1)
    value = (sign * (query + 1)).astype(BF16)
    planes = jnp.arange(NZ, dtype=jnp.int32)
    left = jnp.where(holder_z[:, None] == planes[None, :], value[:, None], jnp.zeros((), BF16))
    right = (lane[:, None] == jnp.arange(SLOTS, dtype=jnp.int32)[None, :]).astype(BF16)
    table = lax.dot_general(left, right, TN, preferred_element_type=F32).astype(BF16)
    row = jnp.concatenate([leaf_target, top_target // 16, top_target % 16, jnp.zeros_like(leaf_target)])
    row = row.astype(BF16)[None, :]
    return jnp.concatenate([queries, table, row, jnp.zeros((TABLE - NZ - 1, D), BF16)], axis=0)


def per_device(queries, shortlist, slab_slot, top_target, leaf_target, top_weight, mid_weight, leaf_weight):
    block = build_block(queries, shortlist, slab_slot, top_target, leaf_target)
    vmem = pl.BlockSpec(memory_space=pltpu.VMEM)
    sem = pltpu.SemaphoreType.DMA
    scratch = [
        pltpu.VMEM((NZ, BLK, D), BF16),
        pltpu.VMEM((NX, 64, D), BF16),
        pltpu.VMEM((272, D), BF16),
        pltpu.VMEM((2, SLOTS, SLOTS), BF16),
        pltpu.VMEM((2, PLANE, ROWS, D), BF16),
        pltpu.VMEM((2, PLANE, ROWS, D), BF16),
        pltpu.VMEM((2, LEAF + 8, SLOTS), F32),
        pltpu.VMEM((2, 256, SLOTS), F32),
        pltpu.VMEM((8, SLOTS), F32),
        pltpu.VMEM((NZ, 128), jnp.int32),
        pltpu.VMEM((NX, 8, 128), F32),
        pltpu.VMEM((PLANE, 8, 128), F32),
        pltpu.VMEM((NX, 8, 128), F32),
        pltpu.VMEM((PLANE, 8, 128), F32),
        pltpu.VMEM((NX, 8, 128), F32),
        pltpu.VMEM((PLANE, 8, 128), F32),
        pltpu.VMEM((3, NZ, 128), F32),
        pltpu.VMEM((NZ, 3, NZ, 128), F32),
        pltpu.VMEM((3, NZ, 128), F32),
        pltpu.VMEM((2, SLOTS, D), F32),
        pltpu.VMEM((2, PLANE, ROWS, D), BF16),
        pltpu.VMEM((2, PLANE, ROWS, D), BF16),
        pltpu.VMEM((PLANE, 8, D), F32),
        pltpu.VMEM((PLANE, 8, D), F32),
        pltpu.VMEM((NZ, 8, 128), F32),
        pltpu.VMEM((NZ, 8, 128), F32),
        pltpu.VMEM((2, 4, QD, D), BF16),
        pltpu.VMEM((2, 4, QD, D), BF16),
        sem((8, PLANE)), sem((8, PLANE)),
        sem((2, 4, 2)), sem((2, 4, 2)),
        sem((2, 4, 2)), sem((2, 4, 2)),
        sem((2, NZ)), sem((2, NZ)),
        sem((NX,)), sem((NX,)),
        sem((NDP,)), sem((NDP,)),
    ]
    query_grad, top_grad, mid_grad, leaf_grad, losses = pl.pallas_call(
        kernel,
        out_shape=(
            jax.ShapeDtypeStruct((QD, D), F32),
            jax.ShapeDtypeStruct((64, D), F32),
            jax.ShapeDtypeStruct((2, D), F32),
            jax.ShapeDtypeStruct((2, LEAF, D), F32),
            jax.ShapeDtypeStruct((3, QD), F32),
        ),
        in_specs=[vmem] * 4,
        out_specs=(vmem,) * 5,
        scratch_shapes=scratch,
        compiler_params=pltpu.CompilerParams(
            collective_id=0, has_side_effects=True, vmem_limit_bytes=48 << 20
        ),
    )(block, leaf_weight, mid_weight, top_weight)
    return query_grad, top_grad, mid_grad, leaf_grad, losses


def solution(mesh):
    both = ("dp", "label")
    in_specs = (
        P(both, None), P(both, None), P(), P(both), P(both),
        P("label", None), P(both, None), P(both, None, None),
    )
    out_specs = (
        P(both, None), P("label", None), P(both, None), P(both, None, None), P(None, both),
    )
    return jax.shard_map(
        per_device, mesh=mesh, in_specs=in_specs, out_specs=out_specs, check_vma=False
    )
```

```python
import jax
import jax.numpy as jnp
from jax import lax
from jax.experimental import pallas as pl
from jax.experimental.pallas import tpu as pltpu
from jax.sharding import PartitionSpec as P

D = 512
BLOCKS = 512
QD = 128
SHORT = 4
LEAF = 128
NZ = 8
NX = 4
NDP = 8
PLANE = NX * NDP
ROWS = 16
SLOTS = PLANE * ROWS
ORDER = (0, 1, 7, 2, 6, 3, 5, 4)
IDX = tuple(ORDER.index(o) for o in range(NZ))
NEG = -1e30
MESH = pl.DeviceIdType.MESH
F32 = jnp.float32
BF16 = jnp.bfloat16
NT = (((1,), (1,)), ((), ()))
TN = (((0,), (0,)), ((), ()))
NN = (((1,), (0,)), ((), ()))


def dot(a, b, dims):
    return lax.dot_general(a, b, dims, preferred_element_type=F32)


def split3(v):
    hi = v.astype(BF16)
    rest = v - hi.astype(F32)
    mid = rest.astype(BF16)
    low = (rest - mid.astype(F32)).astype(BF16)
    return hi, mid, low


def iota(shape, dim):
    return lax.broadcasted_iota(jnp.int32, shape, dim)


def kernel(
    query_in, short_in, slab_in, target_in, leaftarget_in, leaf_in, mid_in, topw_in,
    qg_out, tg_out, mg_out, lg_out, loss_out,
    gq, short_ref, slab_ref, target_ref, leaftarget_ref, mid_ref, tab, tabs,
    xw, wext, oht, slotinfo, pk, rb, sk, ts, cmsg, crecv, emsg, erecv, fmsg, frecv,
    stat, zstat, zlse, tstat, ztop, part, ob, pbk, tgs, tgr, losss, lossr, rsS, rsR,
    qg_ref, tg_ref, mg_ref, lg_ref, loss_ref,
    psend, precv, agsend, agrecv, rssend, rsrecv, zsend, zrecv, wsend, wrecv, osend, orecv, insem, outsem,
):
    dp = lax.axis_index("dp")
    label = lax.axis_index("label")
    x = label // NZ
    z = lax.rem(label, NZ)
    me = x * NDP + dp

    def partner(i):
        tx, td = lax.rem(x + i // NDP, NX), lax.rem(dp + i % NDP, NDP)
        return tx, td

    def plane_id(i):
        tx, td = partner(i)
        return (td, tx * NZ + z)

    def z_id(d):
        return (dp, x * NZ + lax.rem(z + d, NZ))

    def x_id(d):
        return (dp, lax.rem(x + d, NX) * NZ + z)

    def dp_id(d):
        return (lax.rem(dp + d, NDP), label)

    pending = []

    def finish():
        for wait in pending:
            wait()

    barrier = pltpu.get_barrier_semaphore()
    for i in range(1, PLANE):
        pl.semaphore_signal(barrier, inc=1, device_id=plane_id(i), device_id_type=MESH)
    for d in range(1, NZ):
        pl.semaphore_signal(barrier, inc=1, device_id=z_id(d), device_id_type=MESH)

    loads = [
        pltpu.make_async_copy(a, b, insem.at[n])
        for n, (a, b) in enumerate((
            (query_in, gq.at[0]), (short_in, short_ref), (slab_in, slab_ref), (target_in, target_ref),
            (leaftarget_in, leaftarget_ref), (topw_in, xw.at[x]), (mid_in, mid_ref),
            (leaf_in.at[0], wext.at[pl.ds(0, LEAF)]), (leaf_in.at[1], wext.at[pl.ds(LEAF, LEAF)]),
        ))
    ]
    for load in loads:
        load.start()
    loads[0].wait()
    loads[5].wait()
    pl.semaphore_wait(barrier, PLANE - 1 + NZ - 1)

    cuts = ((0, 64), (64, 64))

    def ag(direction, hop, chunk):
        start, length = cuts[chunk]
        if direction == 0:
            src, dst, to = IDX[(NZ - hop + 1) % NZ], IDX[NZ - hop], 1
        else:
            src, dst, to = IDX[hop - 1], IDX[hop], NZ - 1
        rows = pl.ds(start, length)
        return pltpu.make_async_remote_copy(
            src_ref=gq.at[src, rows], dst_ref=gq.at[dst, rows],
            send_sem=agsend.at[direction, hop - 1, chunk],
            recv_sem=agrecv.at[direction, hop - 1, chunk],
            device_id=z_id(to), device_id_type=MESH,
        )

    def ag_start(direction, hop, chunk):
        copy = ag(direction, hop, chunk)
        copy.start()
        pending.append(copy.wait_send)

    def flows(hop):
        return [(0, 0), (1, 1), (1, 0), (0, 1)] if hop < 4 else [(0, 0), (1, 1)]

    for direction, chunk in flows(1):
        ag_start(direction, 1, chunk)

    def wcopy(d, owner):
        return pltpu.make_async_remote_copy(
            src_ref=xw.at[owner], dst_ref=xw.at[owner], send_sem=wsend.at[d], recv_sem=wrecv.at[d],
            device_id=x_id(d), device_id_type=MESH,
        )

    for d in range(1, NX):
        wcopy(d, x).start()
        pending.append(wcopy(d, x).wait_send)

    def remote(phase, source, target, to):
        return pltpu.make_async_remote_copy(
            src_ref=source, dst_ref=target, send_sem=psend.at[phase], recv_sem=precv.at[phase],
            device_id=to, device_id_type=MESH,
        )

    span31 = pl.ds(0, PLANE - 1)
    exchanges = {
        "rows0": (0, lambda tx, td: pk.at[0, tx * NDP + td], rb.at[0]),
        "rows1": (1, lambda tx, td: pk.at[1, tx * NDP + td], rb.at[1]),
        "code": (2, lambda tx, td: cmsg.at[tx], crecv),
        "ex1": (3, lambda tx, td: emsg.at[tx], erecv),
        "ex2": (4, lambda tx, td: fmsg.at[tx], frecv),
        "ret1": (5, lambda tx, td: ob.at[1, tx * NDP + td], pbk.at[1]),
        "ret0": (6, lambda tx, td: ob.at[0, tx * NDP + td], pbk.at[0]),
        "tg": (7, lambda tx, td: tgs.at[tx * NDP + td], tgr),
    }

    def whole(name):
        phase, _, target = exchanges[name]
        return remote(phase, target.at[span31], target.at[span31], plane_id(1))

    def send(name):
        phase, source, target = exchanges[name]
        for i in range(1, PLANE):
            remote(phase, source(*partner(i)), target.at[me], plane_id(i)).start()
        pending.append(whole(name).wait_send)

    def arrived(name):
        whole(name).wait_recv()

    lane = iota((8, 128), 1)

    def regroup(received):
        groups = []
        for g in range(NX):
            out = jnp.zeros((8, 128), F32)
            for j in range(NDP):
                turned = pltpu.roll(received[g * NDP + j], lax.rem(j - dp + NDP, NDP) * ROWS, axis=1)
                out = jnp.where(lane // ROWS == j, turned, out)
            groups.append(out)
        return jnp.concatenate(groups, axis=1)

    for load in loads[1:5]:
        load.wait()
    wide = iota((QD, SLOTS), 1)
    narrow = iota((QD, QD), 1)
    query_col = iota((QD, 1), 0)
    eye = iota((QD, QD), 0) == narrow
    slab = slab_ref[...].astype(F32)
    lower = jnp.where(iota((QD, QD), 1) < iota((QD, QD), 0), 1.0, 0.0).astype(BF16)
    base = jnp.zeros((1, SLOTS), F32)
    table = jnp.zeros((QD, QD), F32)
    for j in range(SHORT):
        named = jnp.sum(jnp.where(eye, short_ref[j : j + 1, :].astype(F32), 0.0), axis=1, keepdims=True).astype(jnp.int32)
        position = jnp.sum(jnp.where(wide == named, slab, 0.0), axis=1, keepdims=True).astype(jnp.int32)
        taken = wide == position
        ones = jnp.where(taken, 1.0, 0.0)
        before = dot(lower, ones.astype(BF16), NN) + base
        base = base + jnp.sum(ones, axis=0, keepdims=True)
        rank = jnp.sum(jnp.where(taken, before, 0.0), axis=1, keepdims=True).astype(jnp.int32)
        holder = position >> 1
        holder_z, holder_x, holder_dp = holder & 7, (holder >> 3) & 3, holder >> 5
        offset = (z - holder_z + NZ) & 7
        index = jnp.zeros((QD, 1), jnp.int32)
        for o in range(NZ):
            index = jnp.where(offset == o, IDX[o], index)
        place = holder_dp * ROWS + (position & 1) * 8 + (index & 3) * 2 + rank
        row = holder_z * NX + holder_x
        left = jnp.where(narrow == row, (query_col + 1).astype(F32), jnp.where(narrow == row + 32, j * 128.0, 0.0))
        right = jnp.where(narrow == place, 1.0, 0.0)
        table = table + dot(left.astype(BF16), right.astype(BF16), TN)
    table = table[0:32] + table[32:64]
    for p in range(NZ):
        tab[p, 0:4, :] = table[4 * p : 4 * p + 4]
        tab[p, 4:5, :] = leaftarget_ref[...].astype(F32)
        tab[p, 5:6, :] = target_ref[...].astype(F32)
        tab[p, 6:8, :] = jnp.zeros((2, 128), F32)

    def tabcopy(d):
        return pltpu.make_async_remote_copy(
            src_ref=tab.at[lax.rem(z + d, NZ)], dst_ref=tabs.at[IDX[NZ - d]], send_sem=zsend.at[2, d],
            recv_sem=zrecv.at[2, d], device_id=z_id(d), device_id_type=MESH,
        )

    for d in range(1, NZ):
        tabcopy(d).start()
        pending.append(tabcopy(d).wait_send)
    tabs[0] = tab[z]

    qid = iota((SLOTS, SLOTS), 0)

    def pack(s):
        ids = jnp.zeros((4, 128), jnp.int32)
        order = jnp.zeros((4, 128), jnp.int32)
        targets = []
        for o4 in range(4):
            tile = tabs[4 * s + o4].astype(jnp.int32)
            value = tile[0:4]
            ids = ids + jnp.where(value > 0, ((value - 1) & 127) + o4 * QD + 1, 0)
            order = order + jnp.where(value > 0, (value - 1) >> 7, 0)
            targets.append(tile[4:5].astype(F32))
        ids = jnp.concatenate([ids[g : g + 1] for g in range(NX)], axis=1)
        order = jnp.concatenate([order[g : g + 1] for g in range(NX)], axis=1)
        live = ids > 0
        hot = jnp.where(qid == ids - 1, 1.0, 0.0).astype(BF16)
        oht[s] = hot
        queries = gq[4 * s : 4 * s + 4].reshape(SLOTS, D)
        pk[s] = dot(hot, queries, TN).astype(BF16).reshape(PLANE, ROWS, D)
        slotinfo[s : s + 1, :] = jnp.where(live, order, -1)
        wanted = jnp.broadcast_to(jnp.concatenate(targets, axis=1), (8, SLOTS)).astype(BF16)
        code = dot(wanted, hot, NN)[0:1, :]
        code = jnp.where(live, jnp.where(order == 0, code, -1.0), -2.0)
        for g in range(NX):
            cmsg[g, s : s + 1, :] = code[:, g * 128 : (g + 1) * 128]

    def top_scores(s):
        queries = gq[4 * s : 4 * s + 4].reshape(SLOTS, D)
        scores = dot(xw[...].reshape(256, D), queries, NT)
        ts[s] = scores
        largest = jnp.max(scores, axis=0, keepdims=True)
        total = largest + jnp.log(jnp.sum(jnp.exp(scores - largest), axis=0, keepdims=True))
        for o4 in range(4):
            o = ORDER[4 * s + o4]
            tstat[o : o + 1, :] = total[:, o4 * 128 : (o4 + 1) * 128]

    for hop in (2, 3):
        for direction, chunk in flows(hop):
            ag(direction, hop - 1, chunk).wait_recv()
            ag_start(direction, hop, chunk)
    for d in range(1, NZ):
        tabcopy(d).wait_recv()
    pack(0)
    send("rows0")
    rb[0, me] = pk[0, me]
    for direction, chunk in flows(4):
        ag(direction, 3, chunk).wait_recv()
        ag_start(direction, 4, chunk)
    for d in range(1, NX):
        wcopy(d, lax.rem(x - d + NX, NX)).wait_recv()
    for load in loads[6:9]:
        load.wait()
    wext[256:272, :] = jnp.concatenate([mid_ref[...].astype(F32), jnp.zeros((14, D), F32)], axis=0).astype(BF16)
    for g in range(NX):
        cmsg[g, 2:8, :] = jnp.zeros((6, 128), F32)
    top_scores(0)
    for direction, chunk in ((1, 0), (0, 1)):
        ag(direction, 3, chunk).wait_recv()
    for direction, chunk in flows(4):
        ag(direction, 4, chunk).wait_recv()
    pack(1)
    send("rows1")
    send("code")
    rb[1, me] = pk[1, me]
    crecv[me] = cmsg[x]
    top_scores(1)

    def zshare(slot, source, target, d):
        return pltpu.make_async_remote_copy(
            src_ref=source, dst_ref=target.at[d], send_sem=zsend.at[slot, d], recv_sem=zrecv.at[slot, d],
            device_id=z_id(d), device_id_type=MESH,
        )

    def share(slot, source, target):
        for d in range(1, NZ):
            zshare(slot, source, target, d).start()
            pending.append(zshare(slot, source, target, d).wait_send)

    def shared(slot, source, target):
        for d in range(1, NZ):
            zshare(slot, source, target, d).wait_recv()

    def joined(own, views):
        views = [own] + [pltpu.roll(view, NZ - d, axis=0) for d, view in views]
        largest = views[0]
        for view in views[1:]:
            largest = jnp.maximum(largest, view)
        total = jnp.zeros((NZ, 128), F32)
        for view in views:
            total = total + jnp.exp(view - largest)
        return largest + jnp.log(total)

    share(3, tstat, ztop)

    odd = (iota((1, SLOTS), 1) >> 3) & 1

    def holder_scores(s):
        scores = dot(wext[...], rb[s].reshape(SLOTS, D), NT)
        sk[s, 0:LEAF, :] = jnp.where(odd == 0, scores[0:LEAF], scores[LEAF : 2 * LEAF])
        sk[s, LEAF : LEAF + 8, :] = jnp.broadcast_to(
            jnp.where(odd == 0, scores[256:257], scores[257:258]), (8, SLOTS)
        )
        chosen = sk[s, 0:LEAF, :]
        largest = jnp.max(chosen, axis=0, keepdims=True)
        total = largest + jnp.log(jnp.sum(jnp.exp(chosen - largest), axis=0, keepdims=True))
        middle = sk[s, LEAF : LEAF + 1, :]
        for g in range(NX):
            span = slice(g * 128, (g + 1) * 128)
            emsg[g, 4 * s : 4 * s + 1, :] = total[:, span]
            emsg[g, 4 * s + 1 : 4 * s + 2, :] = middle[:, span]

    arrived("rows0")
    holder_scores(0)
    arrived("rows1")
    holder_scores(1)
    arrived("code")
    codes = regroup(crecv)
    label_row = iota((LEAF, SLOTS), 0)
    for s in range(2):
        code = codes[s : s + 1, :].astype(jnp.int32)
        target = jnp.sum(jnp.where(label_row == code, sk[s, 0:LEAF, :], 0.0), axis=0, keepdims=True)
        for g in range(NX):
            span = slice(g * 128, (g + 1) * 128)
            emsg[g, 4 * s + 2 : 4 * s + 3, :] = target[:, span]
            emsg[g, 4 * s + 3 : 4 * s + 4, :] = target[:, span]
    send("ex1")
    erecv[me] = emsg[x]

    shared(3, tstat, ztop)
    zlse[2] = joined(tstat[...], [(d, ztop[d]) for d in range(1, NZ)])

    def query_row(which, s):
        return jnp.concatenate([zlse[which, ORDER[4 * s + o4] : ORDER[4 * s + o4] + 1, :] for o4 in range(4)], axis=1)

    weights = xw[...].reshape(256, D)
    class_row = iota((256, SLOTS), 0)
    grad = jnp.zeros((256, D), F32)
    top_losses = []
    for s in range(2):
        scores = ts[s]
        totals = query_row(2, s)
        target = jnp.concatenate([tabs[4 * s + o4, 5:6, :] for o4 in range(4)], axis=1).astype(jnp.int32)
        here = ((target >> 6) & 7) == z
        place = jnp.where(here, ((target >> 9) << 6) + (target & 63), -1)
        hit = class_row == place
        delta = (jnp.exp(scores - totals) - jnp.where(hit, 1.0, 0.0)).astype(BF16)
        score = jnp.sum(jnp.where(hit, scores, 0.0), axis=0, keepdims=True)
        top_losses.append(jnp.where(here, totals - score, 0.0))
        grad = grad + dot(delta, gq[4 * s : 4 * s + 4].reshape(SLOTS, D), NN)
        part[s] = dot(delta, weights, TN)
    tgs[...] = grad.reshape(PLANE, 8, D)

    arrived("ex1")
    pairs = regroup(erecv)
    number = iota((8, SLOTS), 0)
    loss_rows = []
    for s in range(2):
        mine = slotinfo[s : s + 1, :] == number
        leafs = jnp.where(mine, pairs[4 * s : 4 * s + 1, :], 0.0)
        mids = jnp.where(mine, pairs[4 * s + 1 : 4 * s + 2, :], 0.0)
        goal = jnp.where(slotinfo[s : s + 1, :] == 0, pairs[4 * s + 2 : 4 * s + 3, :], 0.0)
        high, mid, low = split3(goal)
        goal = jnp.where(number == 0, high.astype(F32), jnp.where(number == 1, mid.astype(F32), jnp.where(number == 2, low.astype(F32), 0.0)))
        pieces = [piece.astype(F32) for piece in split3(leafs) + split3(mids)]
        pieces = pieces + [jnp.where(mine, 1.0, 0.0), goal]
        rows = dot(jnp.concatenate(pieces, axis=0).astype(BF16), oht[s], NT)
        there = rows[48:56] > 0.5
        leafs = jnp.where(there, rows[0:8] + rows[8:16] + rows[16:24], NEG)
        mids = jnp.where(there, rows[24:32] + rows[32:40] + rows[40:48], NEG)
        loss_rows.append((rows[48:49] > 0.5, rows[56:57] + rows[57:58] + rows[58:59], mids[0:1]))
        for which, values in enumerate((leafs, mids)):
            largest = jnp.max(values, axis=0, keepdims=True)
            total = largest + jnp.log(jnp.sum(jnp.exp(values - largest), axis=0, keepdims=True))
            for o4 in range(4):
                o = ORDER[4 * s + o4]
                stat[which, o : o + 1, :] = total[:, o4 * 128 : (o4 + 1) * 128]

    share(0, stat, zstat)
    send("tg")
    tgr[me] = tgs[me]
    shared(0, stat, zstat)
    for which in range(2):
        zlse[which] = joined(stat[which], [(d, zstat[d, which]) for d in range(1, NZ)])

    for s in range(2):
        pieces = split3(query_row(0, s)) + split3(query_row(1, s))
        pieces = [piece.astype(F32) for piece in pieces] + [jnp.zeros((10, SLOTS), F32)]
        rows = dot(jnp.concatenate(pieces, axis=0).astype(BF16), oht[s], NN)
        leaf_slot = rows[0:1] + rows[1:2] + rows[2:3]
        mid_slot = rows[3:4] + rows[4:5] + rows[5:6]
        for g in range(NX):
            span = slice(g * 128, (g + 1) * 128)
            fmsg[g, 4 * s : 4 * s + 1, :] = leaf_slot[:, span]
            fmsg[g, 4 * s + 1 : 4 * s + 2, :] = mid_slot[:, span]
            fmsg[g, 4 * s + 2 : 4 * s + 3, :] = mid_slot[:, span]
            fmsg[g, 4 * s + 3 : 4 * s + 4, :] = mid_slot[:, span]
    send("ex2")
    frecv[me] = fmsg[x]

    for s in range(2):
        first, goal, middle = loss_rows[s]
        leaf_query = jnp.where(first, query_row(0, s) - goal, 0.0)
        mid_query = jnp.where(first, query_row(1, s) - middle, 0.0)
        for o4 in range(4):
            o = ORDER[4 * s + o4]
            span = slice(o4 * 128, (o4 + 1) * 128)
            losss[o] = jnp.concatenate(
                [top_losses[s][:, span], mid_query[:, span], leaf_query[:, span], jnp.zeros((5, 128), F32)],
                axis=0,
            )

    def losscopy(o):
        return pltpu.make_async_remote_copy(
            src_ref=losss.at[o], dst_ref=lossr.at[o], send_sem=zsend.at[1, o],
            recv_sem=zrecv.at[1, o], device_id=z_id(o), device_id_type=MESH,
        )

    for o in range(1, NZ):
        losscopy(o).start()
        pending.append(losscopy(o).wait_send)

    arrived("ex2")
    scalars = regroup(frecv)
    deltas = []
    for s in (1, 0):
        code = codes[s : s + 1, :].astype(jnp.int32)
        live = code > -2
        hit = jnp.where(label_row == code, 1.0, 0.0)
        delta = jnp.where(live, jnp.exp(sk[s, 0:LEAF, :] - scalars[4 * s : 4 * s + 1, :]) - hit, 0.0)
        middle = jnp.exp(sk[s, LEAF : LEAF + 1, :] - scalars[4 * s + 1 : 4 * s + 2, :])
        middle = jnp.where(live, middle - jnp.where(code >= 0, 1.0, 0.0), 0.0)
        even = odd == 0
        full = jnp.concatenate(
            [
                jnp.where(even, delta, 0.0), jnp.where(even, 0.0, delta),
                jnp.where(even, middle, 0.0), jnp.where(even, 0.0, middle),
                jnp.zeros((14, SLOTS), F32),
            ],
            axis=0,
        ).astype(BF16)
        deltas.append(full)
        ob[s] = dot(full, wext[...], TN).astype(BF16).reshape(PLANE, ROWS, D)
        if s:
            send("ret1")
        pbk[s, me] = ob[s, me]
    arrived("tg")
    tg_sum = tgr[0]
    for f in range(1, PLANE):
        tg_sum = tg_sum + tgr[f]
    tg_ref[pl.ds(pl.multiple_of(dp * 8, 8), 8), :] = tg_sum

    def tgcopy(d, who):
        rows = pl.ds(pl.multiple_of(who * 8, 8), 8)
        return pltpu.make_async_remote_copy(
            src_ref=tg_ref.at[rows], dst_ref=tg_ref.at[rows], send_sem=osend.at[d],
            recv_sem=orecv.at[d], device_id=dp_id(d), device_id_type=MESH,
        )

    for d in range(1, NDP):
        tgcopy(d, dp).start()
        pending.append(tgcopy(d, dp).wait_send)

    halves = (pl.ds(0, 64), pl.ds(64, 64))

    def rs(direction, hop, chunk):
        return pltpu.make_async_remote_copy(
            src_ref=rsS.at[direction, hop, halves[chunk]],
            dst_ref=rsR.at[direction, hop, halves[chunk]],
            send_sem=rssend.at[direction, hop, chunk], recv_sem=rsrecv.at[direction, hop, chunk],
            device_id=z_id(1 if direction == 0 else NZ - 1), device_id_type=MESH,
        )

    def rs_step(direction, hop, chunk):
        o = 4 - hop if direction == 0 else 4 + hop
        index = IDX[o]
        rows = pl.ds((index % 4) * QD + chunk * 64, 64)
        value = part[index // 4, rows, :]
        if hop > 1 or (hop == 1 and chunk == direction):
            rs(direction, hop - 1, chunk).wait_recv()
            value = value + rsR[direction, hop - 1, halves[chunk], :].astype(F32)
        rsS[direction, hop, halves[chunk], :] = value.astype(BF16)
        rs(direction, hop, chunk).start()
        pending.append(rs(direction, hop, chunk).wait_send)

    arrived("ret1")
    send("ret0")
    part[1] = part[1] + dot(oht[1], pbk[1].reshape(SLOTS, D), NN)
    rs_step(0, 0, 0)
    rs_step(1, 0, 1)
    rs_step(0, 1, 1)
    rs_step(1, 1, 0)
    grads = dot(deltas[0], rb[1].reshape(SLOTS, D), NN) + dot(deltas[1], rb[0].reshape(SLOTS, D), NN)
    lg_ref[...] = grads[0:256].reshape(2, LEAF, D)
    mg_ref[...] = grads[256:258]

    def store(n, source, target):
        copy = pltpu.make_async_copy(source, target, outsem.at[n])
        copy.start()
        pending.append(copy.wait)

    store(0, lg_ref, lg_out)
    store(1, mg_ref, mg_out)

    rs_step(0, 1, 0)
    rs_step(1, 1, 1)
    rs_step(1, 2, 0)
    rs_step(1, 2, 1)
    arrived("ret0")
    part[0] = part[0] + dot(oht[0], pbk[0].reshape(SLOTS, D), NN)
    rs_step(0, 2, 1)
    rs_step(0, 2, 0)

    for d in range(1, NDP):
        tgcopy(d, lax.rem(dp - d + NDP, NDP)).wait_recv()
    store(2, tg_ref, tg_out)
    for o in range(1, NZ):
        losscopy(o).wait_recv()
    losses = losss[0]
    for o in range(1, NZ):
        losses = losses + lossr[o]
    loss_ref[...] = losses[0:3]
    store(3, loss_ref, loss_out)

    for direction in range(2):
        for chunk in range(2):
            rs_step(direction, 3, chunk)
    for direction in range(2):
        for chunk in range(2):
            rs(direction, 3, chunk).wait_recv()
    qg_ref[...] = part[0, 0:QD, :] + rsR[0, 3].astype(F32) + rsR[1, 3].astype(F32)
    store(4, qg_ref, qg_out)
    finish()


def place_outputs(*refs):
    for source, target in zip(refs[0:5], refs[5:10]):
        target[...] = source[...]


def per_device(queries, shortlist, slab_slot, top_target, leaf_target, top_weight, mid_weight, leaf_weight):
    hbm = pl.BlockSpec(memory_space=pltpu.HBM)
    vmem = pl.BlockSpec(memory_space=pltpu.VMEM)
    sem = pltpu.SemaphoreType.DMA
    results = (
        jax.ShapeDtypeStruct((QD, D), F32),
        jax.ShapeDtypeStruct((64, D), F32),
        jax.ShapeDtypeStruct((2, D), F32),
        jax.ShapeDtypeStruct((2, LEAF, D), F32),
        jax.ShapeDtypeStruct((3, QD), F32),
    )
    scratch = [
        pltpu.VMEM((NZ, QD, D), BF16),
        pltpu.VMEM((SHORT, QD), jnp.int32),
        pltpu.VMEM((1, BLOCKS), jnp.int32),
        pltpu.VMEM((1, QD), jnp.int32),
        pltpu.VMEM((1, QD), jnp.int32),
        pltpu.VMEM((2, D), BF16),
        pltpu.VMEM((NZ, 8, 128), F32),
        pltpu.VMEM((NZ, 8, 128), F32),
        pltpu.VMEM((NX, 64, D), BF16),
        pltpu.VMEM((272, D), BF16),
        pltpu.VMEM((2, SLOTS, SLOTS), BF16),
        pltpu.VMEM((8, SLOTS), jnp.int32),
        pltpu.VMEM((2, PLANE, ROWS, D), BF16),
        pltpu.VMEM((2, PLANE, ROWS, D), BF16),
        pltpu.VMEM((2, LEAF + 8, SLOTS), F32),
        pltpu.VMEM((2, 256, SLOTS), F32),
        pltpu.VMEM((NX, 8, 128), F32),
        pltpu.VMEM((PLANE, 8, 128), F32),
        pltpu.VMEM((NX, 8, 128), F32),
        pltpu.VMEM((PLANE, 8, 128), F32),
        pltpu.VMEM((NX, 8, 128), F32),
        pltpu.VMEM((PLANE, 8, 128), F32),
        pltpu.VMEM((2, NZ, 128), F32),
        pltpu.VMEM((NZ, 2, NZ, 128), F32),
        pltpu.VMEM((3, NZ, 128), F32),
        pltpu.VMEM((NZ, 128), F32),
        pltpu.VMEM((NZ, NZ, 128), F32),
        pltpu.VMEM((2, SLOTS, D), F32),
        pltpu.VMEM((2, PLANE, ROWS, D), BF16),
        pltpu.VMEM((2, PLANE, ROWS, D), BF16),
        pltpu.VMEM((PLANE, 8, D), F32),
        pltpu.VMEM((PLANE, 8, D), F32),
        pltpu.VMEM((NZ, 8, 128), F32),
        pltpu.VMEM((NZ, 8, 128), F32),
        pltpu.VMEM((2, 4, QD, D), BF16),
        pltpu.VMEM((2, 4, QD, D), BF16),
        *[pltpu.VMEM(result.shape, F32) for result in results],
        sem((8,)), sem((8,)),
        sem((2, 4, 2)), sem((2, 4, 2)),
        sem((2, 4, 2)), sem((2, 4, 2)),
        sem((4, NZ)), sem((4, NZ)),
        sem((NX,)), sem((NX,)),
        sem((NDP,)), sem((NDP,)),
        sem((9,)), sem((5,)),
    ]
    arrays = pl.pallas_call(
        kernel,
        out_shape=results,
        in_specs=[hbm] * 8,
        out_specs=(hbm,) * 5,
        scratch_shapes=scratch,
        compiler_params=pltpu.CompilerParams(
            collective_id=0, has_side_effects=True, vmem_limit_bytes=60 << 20
        ),
    )(
        queries, shortlist.T, slab_slot.reshape(1, -1), top_target.reshape(1, -1), leaf_target.reshape(1, -1),
        leaf_weight, mid_weight, top_weight,
    )
    return pl.pallas_call(
        place_outputs,
        out_shape=results,
        in_specs=[vmem] * 5,
        out_specs=(vmem,) * 5,
        compiler_params=pltpu.CompilerParams(vmem_limit_bytes=60 << 20),
    )(*arrays)


def solution(mesh):
    both = ("dp", "label")
    in_specs = (
        P(both, None), P(both, None), P(), P(both), P(both),
        P("label", None), P(both, None), P(both, None, None),
    )
    out_specs = (
        P(both, None), P("label", None), P(both, None), P(both, None, None), P(None, both),
    )
    return jax.shard_map(
        per_device, mesh=mesh, in_specs=in_specs, out_specs=out_specs, check_vma=False
    )
```

```python
import jax
import jax.numpy as jnp
from jax import lax
from jax.experimental import pallas as pl
from jax.experimental.pallas import tpu as pltpu
from jax.sharding import PartitionSpec as P

D = 512
BLOCKS = 512
QD = 128
SHORT = 4
LEAF = 128
NZ = 8
NX = 4
NDP = 8
PLANE = NX * NDP
STEPS = 4
ROWS = 8
SLOTS = PLANE * ROWS
GROUPS = 2
ORDER = (0, 1, 7, 2, 6, 3, 5, 4)
IDX = tuple(ORDER.index(o) for o in range(NZ))
NEG = -1e30
MESH = pl.DeviceIdType.MESH
F32 = jnp.float32
BF16 = jnp.bfloat16
NT = (((1,), (1,)), ((), ()))
TN = (((0,), (0,)), ((), ()))
NN = (((1,), (0,)), ((), ()))


def dot(a, b, dims):
    return lax.dot_general(a, b, dims, preferred_element_type=F32)


def split3(v):
    hi = v.astype(BF16)
    rest = v - hi.astype(F32)
    mid = rest.astype(BF16)
    low = (rest - mid.astype(F32)).astype(BF16)
    return hi, mid, low


def iota(shape, dim):
    return lax.broadcasted_iota(jnp.int32, shape, dim)


def kernel(
    query_in, short_in, slab_in, target_in, leaftarget_in, leaf_in, mid_in, topw_in,
    qg_out, tg_out, mg_out, lg_out, loss_out,
    gq, short_ref, slab_ref, target_ref, leaftarget_ref, mid_ref, tab, tabs,
    xw, wext, oht, slotinfo, pk, rb, sk, ts, cmsg, crecv, emsg, erecv, gmsg, grecv, fmsg, frecv,
    stat, zstat, zlse, tstat, ztop, part, ob, pbk, tgs, tgx, tgt, tgr, losss, lossr, rsS, rsR,
    qg_ref, tg_ref, mg_ref, lg_ref, loss_ref,
    psend, precv, agsend, agrecv, rssend, rsrecv, zsend, zrecv, wsend, wrecv, osend, orecv, insem, outsem,
):
    dp = lax.axis_index("dp")
    label = lax.axis_index("label")
    x = label // NZ
    z = lax.rem(label, NZ)
    me = x * NDP + dp

    def partner(i):
        tx, td = lax.rem(x + i // NDP, NX), lax.rem(dp + i % NDP, NDP)
        return tx, td

    def plane_id(i):
        tx, td = partner(i)
        return (td, tx * NZ + z)

    def z_id(d):
        return (dp, x * NZ + lax.rem(z + d, NZ))

    def x_id(d):
        return (dp, lax.rem(x + d, NX) * NZ + z)

    def dp_id(d):
        return (lax.rem(dp + d, NDP), label)

    pending = []

    def finish():
        for wait in pending:
            wait()

    barrier = pltpu.get_barrier_semaphore()
    for i in range(1, PLANE):
        pl.semaphore_signal(barrier, inc=1, device_id=plane_id(i), device_id_type=MESH)
    for d in range(1, NZ):
        pl.semaphore_signal(barrier, inc=1, device_id=z_id(d), device_id_type=MESH)

    loads = [
        pltpu.make_async_copy(a, b, insem.at[n])
        for n, (a, b) in enumerate((
            (query_in, gq.at[0]), (short_in, short_ref), (slab_in, slab_ref), (target_in, target_ref),
            (leaftarget_in, leaftarget_ref), (topw_in, xw.at[x]), (mid_in, mid_ref),
            (leaf_in.at[0], wext.at[pl.ds(0, LEAF)]), (leaf_in.at[1], wext.at[pl.ds(LEAF, LEAF)]),
        ))
    ]
    for load in loads:
        load.start()
    loads[0].wait()
    loads[5].wait()
    pl.semaphore_wait(barrier, PLANE - 1 + NZ - 1)

    cuts = ((0, 64), (64, 64))

    def ag(direction, hop, chunk):
        start, length = cuts[chunk]
        if direction == 0:
            src, dst, to = IDX[(NZ - hop + 1) % NZ], IDX[NZ - hop], 1
        else:
            src, dst, to = IDX[hop - 1], IDX[hop], NZ - 1
        rows = pl.ds(start, length)
        return pltpu.make_async_remote_copy(
            src_ref=gq.at[src, rows], dst_ref=gq.at[dst, rows],
            send_sem=agsend.at[direction, hop - 1, chunk],
            recv_sem=agrecv.at[direction, hop - 1, chunk],
            device_id=z_id(to), device_id_type=MESH,
        )

    def ag_start(direction, hop, chunk):
        copy = ag(direction, hop, chunk)
        copy.start()
        pending.append(copy.wait_send)

    def flows(hop):
        return [(0, 0), (1, 1), (1, 0), (0, 1)] if hop < 4 else [(0, 0), (1, 1)]

    for direction, chunk in flows(1):
        ag_start(direction, 1, chunk)

    def wcopy(d, owner):
        return pltpu.make_async_remote_copy(
            src_ref=xw.at[owner], dst_ref=xw.at[owner], send_sem=wsend.at[d], recv_sem=wrecv.at[d],
            device_id=x_id(d), device_id_type=MESH,
        )

    for d in range(1, NX):
        wcopy(d, x).start()
        pending.append(wcopy(d, x).wait_send)

    def remote(phase, source, target, to):
        return pltpu.make_async_remote_copy(
            src_ref=source, dst_ref=target, send_sem=psend.at[phase], recv_sem=precv.at[phase],
            device_id=to, device_id_type=MESH,
        )

    span31 = pl.ds(0, PLANE - 1)
    exchanges = {
        "code": (8, lambda tx, td: cmsg.at[tx // 2], crecv),
        "ex1": (9, lambda tx, td: emsg.at[tx // 2], erecv),
        "goal": (10, lambda tx, td: gmsg.at[tx // 2], grecv),
        "ex2": (11, lambda tx, td: fmsg.at[tx // 2], frecv),
    }
    for t in range(STEPS):
        exchanges[f"rows{t}"] = (t, lambda tx, td, t=t: pk.at[t, tx * NDP + td], rb.at[t])
        exchanges[f"ret{t}"] = (4 + t, lambda tx, td, t=t: ob.at[t, tx * NDP + td], pbk.at[t])

    def whole(name):
        phase, _, target = exchanges[name]
        return remote(phase, target.at[span31], target.at[span31], plane_id(1))

    def send(name):
        phase, source, target = exchanges[name]
        for i in range(1, PLANE):
            remote(phase, source(*partner(i)), target.at[me], plane_id(i)).start()
        pending.append(whole(name).wait_send)

    def arrived(name):
        whole(name).wait_recv()

    lane = iota((8, 128), 1)

    def regroup(received):
        mine = lax.rem(x, 2) * NDP + dp
        groups = []
        for g in range(GROUPS):
            out = jnp.zeros((8, 128), F32)
            for j in range(16):
                turned = pltpu.roll(received[g * 16 + j], lax.rem(j - mine + 16, 16) * ROWS, axis=1)
                out = jnp.where(lane // ROWS == j, turned, out)
            groups.append(out)
        return jnp.concatenate(groups, axis=1)

    def spread(message, row, value):
        for g in range(GROUPS):
            message[g, row : row + 1, :] = value[:, g * 128 : (g + 1) * 128]

    for load in loads[1:5]:
        load.wait()
    wide = iota((QD, BLOCKS), 1)
    narrow = iota((QD, QD), 1)
    query_col = iota((QD, 1), 0)
    eye = iota((QD, QD), 0) == narrow
    slab = slab_ref[...].astype(F32)
    lower = jnp.where(iota((QD, QD), 1) < iota((QD, QD), 0), 1.0, 0.0).astype(BF16)
    base = jnp.zeros((1, BLOCKS), F32)
    table = jnp.zeros((QD, QD), F32)
    for j in range(SHORT):
        named = jnp.sum(jnp.where(eye, short_ref[j : j + 1, :].astype(F32), 0.0), axis=1, keepdims=True).astype(jnp.int32)
        position = jnp.sum(jnp.where(wide == named, slab, 0.0), axis=1, keepdims=True).astype(jnp.int32)
        taken = wide == position
        ones = jnp.where(taken, 1.0, 0.0)
        before = dot(lower, ones.astype(BF16), NN) + base
        base = base + jnp.sum(ones, axis=0, keepdims=True)
        rank = jnp.sum(jnp.where(taken, before, 0.0), axis=1, keepdims=True).astype(jnp.int32)
        holder = position >> 1
        holder_z, holder_x, holder_dp = holder & 7, (holder >> 3) & 3, holder >> 5
        offset = (z - holder_z + NZ) & 7
        index = jnp.zeros((QD, 1), jnp.int32)
        for o in range(NZ):
            index = jnp.where(offset == o, IDX[o], index)
        holder = holder_x * NDP + holder_dp
        place = (holder & 15) * ROWS + (position & 1) * 4 + (index & 1) * 2 + rank
        row = holder_z * 4 + ((index >> 1) & 1) * GROUPS + (holder >> 4)
        left = jnp.where(narrow == row, (query_col + 1).astype(F32), jnp.where(narrow == row + 32, j * 128.0, 0.0))
        right = jnp.where(narrow == place, 1.0, 0.0)
        table = table + dot(left.astype(BF16), right.astype(BF16), TN)
    table = table[0:32] + table[32:64]
    for p in range(NZ):
        tab[p, 0:4, :] = table[4 * p : 4 * p + 4]
        tab[p, 4:5, :] = leaftarget_ref[...].astype(F32)
        tab[p, 5:6, :] = target_ref[...].astype(F32)
        tab[p, 6:8, :] = jnp.zeros((2, 128), F32)

    def tabcopy(d):
        return pltpu.make_async_remote_copy(
            src_ref=tab.at[lax.rem(z + d, NZ)], dst_ref=tabs.at[IDX[NZ - d]], send_sem=zsend.at[2, d],
            recv_sem=zrecv.at[2, d], device_id=z_id(d), device_id_type=MESH,
        )

    for d in range(1, NZ):
        tabcopy(d).start()
        pending.append(tabcopy(d).wait_send)
    tabs[0] = tab[z]

    qid = iota((SLOTS, SLOTS), 0)

    def queries_of(t):
        return gq[2 * t : 2 * t + 2].reshape(SLOTS, D)

    def pack(t):
        ids = jnp.zeros((GROUPS, 128), jnp.int32)
        order = jnp.zeros((GROUPS, 128), jnp.int32)
        targets = []
        half = GROUPS * (t % 2)
        for o2 in range(2):
            tile = tabs[2 * t + o2].astype(jnp.int32)
            value = tile[half : half + GROUPS]
            ids = ids + jnp.where(value > 0, ((value - 1) & 127) + o2 * QD + 1, 0)
            order = order + jnp.where(value > 0, (value - 1) >> 7, 0)
            targets.append(tile[4:5].astype(F32))
        ids = jnp.concatenate([ids[g : g + 1] for g in range(GROUPS)], axis=1)
        order = jnp.concatenate([order[g : g + 1] for g in range(GROUPS)], axis=1)
        live = ids > 0
        hot = jnp.where(qid == ids - 1, 1.0, 0.0).astype(BF16)
        oht[t] = hot
        pk[t] = dot(hot, queries_of(t), TN).astype(BF16).reshape(PLANE, ROWS, D)
        send(f"rows{t}")
        rb[t, me] = pk[t, me]
        slotinfo[t : t + 1, :] = jnp.where(live, order, -1)
        wanted = jnp.broadcast_to(jnp.concatenate(targets, axis=1), (8, SLOTS)).astype(BF16)
        code = dot(wanted, hot, NN)[0:1, :]
        spread(cmsg, t, jnp.where(live, jnp.where(order == 0, code, -1.0), -2.0))

    def top_scores(t):
        scores = dot(xw[...].reshape(256, D), queries_of(t), NT)
        ts[t] = scores
        largest = jnp.max(scores, axis=0, keepdims=True)
        total = largest + jnp.log(jnp.sum(jnp.exp(scores - largest), axis=0, keepdims=True))
        for o2 in range(2):
            o = ORDER[2 * t + o2]
            tstat[o : o + 1, :] = total[:, o2 * 128 : (o2 + 1) * 128]

    def forward(hop, direction):
        for chunk in range(2):
            if hop < 4 or chunk == direction:
                ag(direction, hop - 1, chunk).wait_recv()
                ag_start(direction, hop, chunk)

    for direction in range(2):
        forward(2, direction)
    for d in range(1, NZ):
        tabcopy(d).wait_recv()
    pack(0)
    for direction in range(2):
        forward(3, direction)
    pack(1)
    for d in range(1, NX):
        wcopy(d, lax.rem(x - d + NX, NX)).wait_recv()
    top_scores(0)
    for direction in range(2):
        forward(4, direction)
    ag(1, 3, 0).wait_recv()
    pack(2)
    for load in loads[6:9]:
        load.wait()
    wext[256:272, :] = jnp.concatenate([mid_ref[...].astype(F32), jnp.zeros((14, D), F32)], axis=0).astype(BF16)
    for g in range(GROUPS):
        cmsg[g, 4:8, :] = jnp.zeros((4, 128), F32)
        gmsg[g, 4:8, :] = jnp.zeros((4, 128), F32)
    top_scores(1)
    ag(0, 3, 1).wait_recv()
    for direction, chunk in flows(4):
        ag(direction, 4, chunk).wait_recv()
    pack(3)
    send("code")
    crecv[me] = cmsg[x // 2]
    top_scores(2)
    top_scores(3)

    def zshare(slot, source, target, d):
        return pltpu.make_async_remote_copy(
            src_ref=source, dst_ref=target.at[d], send_sem=zsend.at[slot, d], recv_sem=zrecv.at[slot, d],
            device_id=z_id(d), device_id_type=MESH,
        )

    def share(slot, source, target):
        for d in range(1, NZ):
            zshare(slot, source, target, d).start()
            pending.append(zshare(slot, source, target, d).wait_send)

    def shared(slot, source, target):
        for d in range(1, NZ):
            zshare(slot, source, target, d).wait_recv()

    def joined(own, views):
        views = [own] + [pltpu.roll(view, NZ - d, axis=0) for d, view in views]
        largest = views[0]
        for view in views[1:]:
            largest = jnp.maximum(largest, view)
        total = jnp.zeros((NZ, 128), F32)
        for view in views:
            total = total + jnp.exp(view - largest)
        return largest + jnp.log(total)

    share(3, tstat, ztop)

    odd = (iota((1, SLOTS), 1) >> 2) & 1

    def holder_scores(s):
        scores = dot(wext[...], rb[s].reshape(SLOTS, D), NT)
        sk[s, 0:LEAF, :] = jnp.where(odd == 0, scores[0:LEAF], scores[LEAF : 2 * LEAF])
        sk[s, LEAF : LEAF + 8, :] = jnp.broadcast_to(
            jnp.where(odd == 0, scores[256:257], scores[257:258]), (8, SLOTS)
        )
        chosen = sk[s, 0:LEAF, :]
        largest = jnp.max(chosen, axis=0, keepdims=True)
        total = largest + jnp.log(jnp.sum(jnp.exp(chosen - largest), axis=0, keepdims=True))
        spread(emsg, 2 * s, total)
        spread(emsg, 2 * s + 1, sk[s, LEAF : LEAF + 1, :])

    for t in range(STEPS):
        arrived(f"rows{t}")
        holder_scores(t)
    send("ex1")
    erecv[me] = emsg[x // 2]
    arrived("code")
    codes = regroup(crecv)
    label_row = iota((LEAF, SLOTS), 0)
    for t in range(STEPS):
        code = codes[t : t + 1, :].astype(jnp.int32)
        spread(gmsg, t, jnp.sum(jnp.where(label_row == code, sk[t, 0:LEAF, :], 0.0), axis=0, keepdims=True))

    shared(3, tstat, ztop)
    zlse[2] = joined(tstat[...], [(d, ztop[d]) for d in range(1, NZ)])

    def query_row(which, t):
        return jnp.concatenate([zlse[which, ORDER[2 * t + o2] : ORDER[2 * t + o2] + 1, :] for o2 in range(2)], axis=1)

    weights = xw[...].reshape(256, D)
    class_row = iota((256, SLOTS), 0)
    grad = jnp.zeros((256, D), F32)
    top_losses = []
    for t in range(STEPS):
        scores = ts[t]
        totals = query_row(2, t)
        target = jnp.concatenate([tabs[2 * t + o2, 5:6, :] for o2 in range(2)], axis=1).astype(jnp.int32)
        here = ((target >> 6) & 7) == z
        place = jnp.where(here, ((target >> 9) << 6) + (target & 63), -1)
        hit = class_row == place
        delta = (jnp.exp(scores - totals) - jnp.where(hit, 1.0, 0.0)).astype(BF16)
        score = jnp.sum(jnp.where(hit, scores, 0.0), axis=0, keepdims=True)
        top_losses.append(jnp.where(here, totals - score, 0.0))
        grad = grad + dot(delta, queries_of(t), NN)
        part[t] = dot(delta, weights, TN)
    core = lax.rem(dp, 2)
    for p in range(PLANE):
        tgs[p % 2, p // 2] = grad[8 * p : 8 * p + 8]
    pair_copy = pltpu.make_async_remote_copy(
        src_ref=tgs.at[1 - core], dst_ref=tgx, send_sem=osend.at[0], recv_sem=orecv.at[0],
        device_id=(dp + 1 - 2 * core, label), device_id_type=MESH,
    )
    pair_copy.start()
    pending.append(pair_copy.wait_send)

    def tg_partner(i):
        return lax.rem(x + i // 4, NX), lax.rem(dp // 2 + i % 4, 4)

    def tg_remote(source, target, i):
        tx, ty = tg_partner(i)
        return pltpu.make_async_remote_copy(
            src_ref=source, dst_ref=target, send_sem=psend.at[12], recv_sem=precv.at[12],
            device_id=(ty * 2 + core, tx * NZ + z), device_id_type=MESH,
        )

    tg_whole = tg_remote(tgr.at[pl.ds(0, 15)], tgr.at[pl.ds(0, 15)], 1)

    arrived("ex1")
    pairs = regroup(erecv)
    number = iota((8, SLOTS), 0)
    loss_rows = []
    for t in range(STEPS):
        mine = slotinfo[t : t + 1, :] == number
        leafs = jnp.where(mine, pairs[2 * t : 2 * t + 1, :], 0.0)
        mids = jnp.where(mine, pairs[2 * t + 1 : 2 * t + 2, :], 0.0)
        pieces = [piece.astype(F32) for piece in split3(leafs) + split3(mids)]
        pieces = pieces + [jnp.where(mine, 1.0, 0.0), jnp.zeros((8, SLOTS), F32)]
        rows = dot(jnp.concatenate(pieces, axis=0).astype(BF16), oht[t], NT)
        there = rows[48:56] > 0.5
        leafs = jnp.where(there, rows[0:8] + rows[8:16] + rows[16:24], NEG)
        mids = jnp.where(there, rows[24:32] + rows[32:40] + rows[40:48], NEG)
        loss_rows.append((there[0:1], mids[0:1]))
        for which, values in enumerate((leafs, mids)):
            largest = jnp.max(values, axis=0, keepdims=True)
            total = largest + jnp.log(jnp.sum(jnp.exp(values - largest), axis=0, keepdims=True))
            for o2 in range(2):
                o = ORDER[2 * t + o2]
                stat[which, o : o + 1, :] = total[:, o2 * 128 : (o2 + 1) * 128]

    share(0, stat, zstat)
    pair_copy.wait_recv()
    own = x * 4 + dp // 2
    tgt[...] = tgs[core] + tgx[...]
    for i in range(1, 16):
        tx, ty = tg_partner(i)
        tg_remote(tgt.at[tx * 4 + ty], tgr.at[own], i).start()
    pending.append(tg_whole.wait_send)
    tgr[own] = tgt[own]
    shared(0, stat, zstat)
    for which in range(2):
        zlse[which] = joined(stat[which], [(d, zstat[d, which]) for d in range(1, NZ)])

    for t in range(STEPS):
        pieces = split3(query_row(0, t)) + split3(query_row(1, t))
        pieces = [piece.astype(F32) for piece in pieces] + [jnp.zeros((10, SLOTS), F32)]
        rows = dot(jnp.concatenate(pieces, axis=0).astype(BF16), oht[t], NN)
        spread(fmsg, 2 * t, rows[0:1] + rows[1:2] + rows[2:3])
        spread(fmsg, 2 * t + 1, rows[3:4] + rows[4:5] + rows[5:6])
    send("ex2")
    frecv[me] = fmsg[x // 2]
    send("goal")
    grecv[me] = gmsg[x // 2]

    def losscopy(o):
        return pltpu.make_async_remote_copy(
            src_ref=losss.at[o], dst_ref=lossr.at[o], send_sem=zsend.at[1, o],
            recv_sem=zrecv.at[1, o], device_id=z_id(o), device_id_type=MESH,
        )

    arrived("ex2")
    scalars = regroup(frecv)
    even = odd == 0
    deltas = [None] * STEPS

    def back_rows(t):
        code = codes[t : t + 1, :].astype(jnp.int32)
        live = code > -2
        hit = jnp.where(label_row == code, 1.0, 0.0)
        delta = jnp.where(live, jnp.exp(sk[t, 0:LEAF, :] - scalars[2 * t : 2 * t + 1, :]) - hit, 0.0)
        middle = jnp.exp(sk[t, LEAF : LEAF + 1, :] - scalars[2 * t + 1 : 2 * t + 2, :])
        middle = jnp.where(live, middle - jnp.where(code >= 0, 1.0, 0.0), 0.0)
        full = jnp.concatenate(
            [
                jnp.where(even, delta, 0.0), jnp.where(even, 0.0, delta),
                jnp.where(even, middle, 0.0), jnp.where(even, 0.0, middle),
                jnp.zeros((14, SLOTS), F32),
            ],
            axis=0,
        ).astype(BF16)
        deltas[t] = full
        ob[t] = dot(full, wext[...], TN).astype(BF16).reshape(PLANE, ROWS, D)

    def send_back(t):
        send(f"ret{t}")
        pbk[t, me] = ob[t, me]

    for t in (3, 2, 1, 0):
        back_rows(t)
        send_back(t)

    tg_whole.wait_recv()
    tg_sum = tgr[0]
    for f in range(1, PLANE // 2):
        tg_sum = tg_sum + tgr[f]
    tg_ref[pl.ds(pl.multiple_of(dp * 8, 8), 8), :] = tg_sum

    def tgcopy(d, who):
        rows = pl.ds(pl.multiple_of(who * 8, 8), 8)
        return pltpu.make_async_remote_copy(
            src_ref=tg_ref.at[rows], dst_ref=tg_ref.at[rows], send_sem=osend.at[d],
            recv_sem=orecv.at[d], device_id=dp_id(d), device_id_type=MESH,
        )

    for d in range(1, NDP):
        tgcopy(d, dp).start()
        pending.append(tgcopy(d, dp).wait_send)

    def send_losses():
        arrived("goal")
        goals = regroup(grecv)
        for t in range(STEPS):
            goal = jnp.where(slotinfo[t : t + 1, :] == 0, goals[t : t + 1, :], 0.0)
            pieces = [piece.astype(F32) for piece in split3(goal)] + [jnp.zeros((13, SLOTS), F32)]
            rows = dot(jnp.concatenate(pieces, axis=0).astype(BF16), oht[t], NT)
            first, middle = loss_rows[t]
            leaf_query = jnp.where(first, query_row(0, t) - (rows[0:1] + rows[1:2] + rows[2:3]), 0.0)
            mid_query = jnp.where(first, query_row(1, t) - middle, 0.0)
            for o2 in range(2):
                o = ORDER[2 * t + o2]
                span = slice(o2 * 128, (o2 + 1) * 128)
                losss[o] = jnp.concatenate(
                    [top_losses[t][:, span], mid_query[:, span], leaf_query[:, span], jnp.zeros((5, 128), F32)],
                    axis=0,
                )
        for o in range(1, NZ):
            losscopy(o).start()
            pending.append(losscopy(o).wait_send)


    def store(n, source, target):
        copy = pltpu.make_async_copy(source, target, outsem.at[n])
        copy.start()
        pending.append(copy.wait)

    halves = (pl.ds(0, 64), pl.ds(64, 64))

    def rs(direction, hop, chunk):
        return pltpu.make_async_remote_copy(
            src_ref=rsS.at[direction, hop, halves[chunk]],
            dst_ref=rsR.at[direction, hop, halves[chunk]],
            send_sem=rssend.at[direction, hop, chunk], recv_sem=rsrecv.at[direction, hop, chunk],
            device_id=z_id(1 if direction == 0 else NZ - 1), device_id_type=MESH,
        )

    def rs_step(direction, hop, chunk):
        o = 4 - hop if direction == 0 else 4 + hop
        index = IDX[o]
        rows = pl.ds((index % 2) * QD + chunk * 64, 64)
        value = part[index // 2, rows, :]
        if hop > 1 or (hop == 1 and chunk == direction):
            rs(direction, hop - 1, chunk).wait_recv()
            value = value + rsR[direction, hop - 1, halves[chunk], :].astype(F32)
        rsS[direction, hop, halves[chunk], :] = value.astype(BF16)
        rs(direction, hop, chunk).start()
        pending.append(rs(direction, hop, chunk).wait_send)

    def returned(t):
        arrived(f"ret{t}")
        part[t] = part[t] + dot(oht[t], pbk[t].reshape(SLOTS, D), NN)

    returned(3)
    rs_step(0, 0, 0)
    rs_step(1, 0, 1)
    rs_step(1, 1, 0)
    returned(2)
    rs_step(0, 1, 1)
    rs_step(1, 1, 1)
    rs_step(0, 1, 0)
    rs_step(1, 2, 0)
    send_losses()
    rs_step(1, 2, 1)
    returned(1)
    rs_step(0, 2, 1)
    rs_step(1, 3, 0)
    rs_step(0, 2, 0)
    rs_step(1, 3, 1)
    grads = jnp.zeros((272, D), F32)
    for t in range(STEPS):
        grads = grads + dot(deltas[t], rb[t].reshape(SLOTS, D), NN)
    lg_ref[...] = grads[0:256].reshape(2, LEAF, D)
    mg_ref[...] = grads[256:258]
    store(0, lg_ref, lg_out)
    store(1, mg_ref, mg_out)
    returned(0)
    rs_step(0, 3, 1)
    rs_step(0, 3, 0)

    for d in range(1, NDP):
        tgcopy(d, lax.rem(dp - d + NDP, NDP)).wait_recv()
    store(2, tg_ref, tg_out)
    for o in range(1, NZ):
        losscopy(o).wait_recv()
    losses = losss[0]
    for o in range(1, NZ):
        losses = losses + lossr[o]
    loss_ref[...] = losses[0:3]
    store(3, loss_ref, loss_out)
    for chunk in (0, 1):
        rs(1, 3, chunk).wait_recv()
    for chunk in (1, 0):
        rs(0, 3, chunk).wait_recv()
    qg_ref[...] = part[0, 0:QD, :] + rsR[0, 3].astype(F32) + rsR[1, 3].astype(F32)
    store(4, qg_ref, qg_out)
    finish()


def place_outputs(*refs):
    for source, target in zip(refs[0:5], refs[5:10]):
        target[...] = source[...]


def per_device(queries, shortlist, slab_slot, top_target, leaf_target, top_weight, mid_weight, leaf_weight):
    hbm = pl.BlockSpec(memory_space=pltpu.HBM)
    vmem = pl.BlockSpec(memory_space=pltpu.VMEM)
    sem = pltpu.SemaphoreType.DMA
    results = (
        jax.ShapeDtypeStruct((QD, D), F32),
        jax.ShapeDtypeStruct((64, D), F32),
        jax.ShapeDtypeStruct((2, D), F32),
        jax.ShapeDtypeStruct((2, LEAF, D), F32),
        jax.ShapeDtypeStruct((3, QD), F32),
    )
    scratch = [
        pltpu.VMEM((NZ, QD, D), BF16),
        pltpu.VMEM((SHORT, QD), jnp.int32),
        pltpu.VMEM((1, BLOCKS), jnp.int32),
        pltpu.VMEM((1, QD), jnp.int32),
        pltpu.VMEM((1, QD), jnp.int32),
        pltpu.VMEM((2, D), BF16),
        pltpu.VMEM((NZ, 8, 128), F32),
        pltpu.VMEM((NZ, 8, 128), F32),
        pltpu.VMEM((NX, 64, D), BF16),
        pltpu.VMEM((272, D), BF16),
        pltpu.VMEM((STEPS, SLOTS, SLOTS), BF16),
        pltpu.VMEM((8, SLOTS), jnp.int32),
        pltpu.VMEM((STEPS, PLANE, ROWS, D), BF16),
        pltpu.VMEM((STEPS, PLANE, ROWS, D), BF16),
        pltpu.VMEM((STEPS, LEAF + 8, SLOTS), F32),
        pltpu.VMEM((STEPS, 256, SLOTS), F32),
        pltpu.VMEM((GROUPS, 8, 128), F32),
        pltpu.VMEM((PLANE, 8, 128), F32),
        pltpu.VMEM((GROUPS, 8, 128), F32),
        pltpu.VMEM((PLANE, 8, 128), F32),
        pltpu.VMEM((GROUPS, 8, 128), F32),
        pltpu.VMEM((PLANE, 8, 128), F32),
        pltpu.VMEM((GROUPS, 8, 128), F32),
        pltpu.VMEM((PLANE, 8, 128), F32),
        pltpu.VMEM((2, NZ, 128), F32),
        pltpu.VMEM((NZ, 2, NZ, 128), F32),
        pltpu.VMEM((3, NZ, 128), F32),
        pltpu.VMEM((NZ, 128), F32),
        pltpu.VMEM((NZ, NZ, 128), F32),
        pltpu.VMEM((STEPS, SLOTS, D), F32),
        pltpu.VMEM((STEPS, PLANE, ROWS, D), BF16),
        pltpu.VMEM((STEPS, PLANE, ROWS, D), BF16),
        pltpu.VMEM((2, PLANE // 2, 8, D), F32),
        pltpu.VMEM((PLANE // 2, 8, D), F32),
        pltpu.VMEM((PLANE // 2, 8, D), F32),
        pltpu.VMEM((PLANE // 2, 8, D), F32),
        pltpu.VMEM((NZ, 8, 128), F32),
        pltpu.VMEM((NZ, 8, 128), F32),
        pltpu.VMEM((2, 4, QD, D), BF16),
        pltpu.VMEM((2, 4, QD, D), BF16),
        *[pltpu.VMEM(result.shape, F32) for result in results],
        sem((13,)), sem((13,)),
        sem((2, 4, 2)), sem((2, 4, 2)),
        sem((2, 4, 2)), sem((2, 4, 2)),
        sem((4, NZ)), sem((4, NZ)),
        sem((NX,)), sem((NX,)),
        sem((NDP,)), sem((NDP,)),
        sem((9,)), sem((5,)),
    ]
    arrays = pl.pallas_call(
        kernel,
        out_shape=results,
        in_specs=[hbm] * 8,
        out_specs=(hbm,) * 5,
        scratch_shapes=scratch,
        compiler_params=pltpu.CompilerParams(
            collective_id=0, has_side_effects=True, vmem_limit_bytes=60 << 20
        ),
    )(
        queries, shortlist.T, slab_slot.reshape(1, -1), top_target.reshape(1, -1), leaf_target.reshape(1, -1),
        leaf_weight, mid_weight, top_weight,
    )
    return pl.pallas_call(
        place_outputs,
        out_shape=results,
        in_specs=[vmem] * 5,
        out_specs=(vmem,) * 5,
        compiler_params=pltpu.CompilerParams(vmem_limit_bytes=60 << 20),
    )(*arrays)


def solution(mesh):
    both = ("dp", "label")
    in_specs = (
        P(both, None), P(both, None), P(), P(both), P(both),
        P("label", None), P(both, None), P(both, None, None),
    )
    out_specs = (
        P(both, None), P("label", None), P(both, None), P(both, None, None), P(None, both),
    )
    return jax.shard_map(
        per_device, mesh=mesh, in_specs=in_specs, out_specs=out_specs, check_vma=False
    )
```

```python
import jax
import jax.numpy as jnp
from jax import lax
from jax.experimental import pallas as pl
from jax.experimental.pallas import tpu as pltpu
from jax.sharding import PartitionSpec as P

D = 512
BLOCKS = 512
QD = 128
SHORT = 4
LEAF = 128
NZ = 8
NX = 4
NDP = 8
PLANE = NX * NDP
STEPS = 4
ROWS = 8
SLOTS = PLANE * ROWS
GROUPS = 2
ORDER = (0, 1, 7, 2, 6, 3, 5, 4)
IDX = tuple(ORDER.index(o) for o in range(NZ))
NEG = -1e30
MESH = pl.DeviceIdType.MESH
F32 = jnp.float32
BF16 = jnp.bfloat16
NT = (((1,), (1,)), ((), ()))
TN = (((0,), (0,)), ((), ()))
NN = (((1,), (0,)), ((), ()))


def dot(a, b, dims):
    return lax.dot_general(a, b, dims, preferred_element_type=F32)


def split3(v):
    hi = v.astype(BF16)
    rest = v - hi.astype(F32)
    mid = rest.astype(BF16)
    low = (rest - mid.astype(F32)).astype(BF16)
    return hi, mid, low


def iota(shape, dim):
    return lax.broadcasted_iota(jnp.int32, shape, dim)


def kernel(
    query_in, short_in, slab_in, target_in, leaftarget_in, leaf_in, mid_in, topw_in,
    qg_out, tg_out, mg_out, lg_out, loss_out,
    gq, short_ref, slab_ref, target_ref, leaftarget_ref, mid_ref, tab, tabs,
    xw, wext, oht, slotinfo, pk, rb, sk, ts, cmsg, crecv, emsg, erecv, gmsg, grecv, fmsg, frecv,
    stat, zstat, zlse, tstat, ztop, part, ob, pbk, tgs, tgx, tgt, tgr, losss, lossr, rsS, rsR,
    qg_ref, tg_ref, mg_ref, lg_ref, loss_ref,
    psend, precv, agsend, agrecv, rssend, rsrecv, zsend, zrecv, wsend, wrecv, osend, orecv, insem, outsem,
):
    dp = lax.axis_index("dp")
    label = lax.axis_index("label")
    x = label // NZ
    z = lax.rem(label, NZ)
    me = x * NDP + dp

    def partner(i):
        tx, td = lax.rem(x + i // NDP, NX), lax.rem(dp + i % NDP, NDP)
        return tx, td

    def plane_id(i):
        tx, td = partner(i)
        return (td, tx * NZ + z)

    def z_id(d):
        return (dp, x * NZ + lax.rem(z + d, NZ))

    def x_id(d):
        return (dp, lax.rem(x + d, NX) * NZ + z)

    def dp_id(d):
        return (lax.rem(dp + d, NDP), label)

    pending = []

    def finish():
        for wait in pending:
            wait()

    barrier = pltpu.get_barrier_semaphore()
    for i in range(1, PLANE):
        pl.semaphore_signal(barrier, inc=1, device_id=plane_id(i), device_id_type=MESH)
    for d in range(1, NZ):
        pl.semaphore_signal(barrier, inc=1, device_id=z_id(d), device_id_type=MESH)

    loads = [
        pltpu.make_async_copy(a, b, insem.at[n])
        for n, (a, b) in enumerate((
            (query_in, gq.at[0]), (short_in, short_ref), (slab_in, slab_ref), (target_in, target_ref),
            (leaftarget_in, leaftarget_ref), (topw_in, xw.at[x]), (mid_in, mid_ref),
            (leaf_in.at[0], wext.at[pl.ds(0, LEAF)]), (leaf_in.at[1], wext.at[pl.ds(LEAF, LEAF)]),
        ))
    ]
    for load in loads:
        load.start()
    loads[0].wait()
    loads[5].wait()
    pl.semaphore_wait(barrier, PLANE - 1 + NZ - 1)

    cuts = ((0, 64), (64, 64))

    def ag(direction, hop, chunk):
        start, length = cuts[chunk]
        if direction == 0:
            src, dst, to = IDX[(NZ - hop + 1) % NZ], IDX[NZ - hop], 1
        else:
            src, dst, to = IDX[hop - 1], IDX[hop], NZ - 1
        rows = pl.ds(start, length)
        return pltpu.make_async_remote_copy(
            src_ref=gq.at[src, rows], dst_ref=gq.at[dst, rows],
            send_sem=agsend.at[direction, hop - 1, chunk],
            recv_sem=agrecv.at[direction, hop - 1, chunk],
            device_id=z_id(to), device_id_type=MESH,
        )

    def ag_start(direction, hop, chunk):
        copy = ag(direction, hop, chunk)
        copy.start()
        pending.append(copy.wait_send)

    def flows(hop):
        return [(0, 0), (1, 1), (0, 1), (1, 0)] if hop < 4 else [(0, 0), (1, 1)]

    for direction, chunk in flows(1):
        ag_start(direction, 1, chunk)

    def wcopy(d, owner):
        return pltpu.make_async_remote_copy(
            src_ref=xw.at[owner], dst_ref=xw.at[owner], send_sem=wsend.at[d], recv_sem=wrecv.at[d],
            device_id=x_id(d), device_id_type=MESH,
        )

    for d in range(1, NX):
        wcopy(d, x).start()
        pending.append(wcopy(d, x).wait_send)

    def remote(phase, source, target, to):
        return pltpu.make_async_remote_copy(
            src_ref=source, dst_ref=target, send_sem=psend.at[phase], recv_sem=precv.at[phase],
            device_id=to, device_id_type=MESH,
        )

    span31 = pl.ds(0, PLANE - 1)
    exchanges = {
        "code": (8, lambda tx, td: cmsg.at[tx // 2], crecv),
        "ex1": (9, lambda tx, td: emsg.at[tx // 2], erecv),
        "goal": (10, lambda tx, td: gmsg.at[tx // 2], grecv),
        "ex2": (11, lambda tx, td: fmsg.at[tx // 2], frecv),
    }
    for t in range(STEPS):
        exchanges[f"rows{t}"] = (t, lambda tx, td, t=t: pk.at[t, tx * NDP + td], rb.at[t])
        exchanges[f"ret{t}"] = (4 + t, lambda tx, td, t=t: ob.at[t, tx * NDP + td], pbk.at[t])

    def whole(name):
        phase, _, target = exchanges[name]
        return remote(phase, target.at[span31], target.at[span31], plane_id(1))

    def send(name):
        phase, source, target = exchanges[name]
        for i in range(1, PLANE):
            remote(phase, source(*partner(i)), target.at[me], plane_id(i)).start()
        pending.append(whole(name).wait_send)

    def arrived(name):
        whole(name).wait_recv()

    lane = iota((8, 128), 1)

    def regroup(received):
        mine = lax.rem(x, 2) * NDP + dp
        groups = []
        for g in range(GROUPS):
            out = jnp.zeros((8, 128), F32)
            for j in range(16):
                turned = pltpu.roll(received[g * 16 + j], lax.rem(j - mine + 16, 16) * ROWS, axis=1)
                out = jnp.where(lane // ROWS == j, turned, out)
            groups.append(out)
        return jnp.concatenate(groups, axis=1)

    def spread(message, row, value):
        for g in range(GROUPS):
            message[g, row : row + 1, :] = value[:, g * 128 : (g + 1) * 128]

    for load in loads[1:5]:
        load.wait()
    wide = iota((QD, BLOCKS), 1)
    narrow = iota((QD, QD), 1)
    query_col = iota((QD, 1), 0)
    eye = iota((QD, QD), 0) == narrow
    slab = slab_ref[...].astype(F32)
    lower = jnp.where(iota((QD, QD), 1) < iota((QD, QD), 0), 1.0, 0.0).astype(BF16)
    base = jnp.zeros((1, BLOCKS), F32)
    table = jnp.zeros((QD, QD), F32)
    for j in range(SHORT):
        named = jnp.sum(jnp.where(eye, short_ref[j : j + 1, :].astype(F32), 0.0), axis=1, keepdims=True).astype(jnp.int32)
        position = jnp.sum(jnp.where(wide == named, slab, 0.0), axis=1, keepdims=True).astype(jnp.int32)
        taken = wide == position
        ones = jnp.where(taken, 1.0, 0.0)
        before = dot(lower, ones.astype(BF16), NN) + base
        base = base + jnp.sum(ones, axis=0, keepdims=True)
        rank = jnp.sum(jnp.where(taken, before, 0.0), axis=1, keepdims=True).astype(jnp.int32)
        holder = position >> 1
        holder_z, holder_x, holder_dp = holder & 7, (holder >> 3) & 3, holder >> 5
        offset = (z - holder_z + NZ) & 7
        index = jnp.zeros((QD, 1), jnp.int32)
        for o in range(NZ):
            index = jnp.where(offset == o, IDX[o], index)
        holder = holder_x * NDP + holder_dp
        place = (holder & 15) * ROWS + (position & 1) * 4 + (index & 1) * 2 + rank
        row = holder_z * 4 + ((index >> 1) & 1) * GROUPS + (holder >> 4)
        left = jnp.where(narrow == row, (query_col + 1).astype(F32), jnp.where(narrow == row + 32, j * 128.0, 0.0))
        right = jnp.where(narrow == place, 1.0, 0.0)
        table = table + dot(left.astype(BF16), right.astype(BF16), TN)
    table = table[0:32] + table[32:64]
    for p in range(NZ):
        tab[p, 0:4, :] = table[4 * p : 4 * p + 4]
        tab[p, 4:5, :] = leaftarget_ref[...].astype(F32)
        tab[p, 5:6, :] = target_ref[...].astype(F32)
        tab[p, 6:8, :] = jnp.zeros((2, 128), F32)

    def tabcopy(d):
        return pltpu.make_async_remote_copy(
            src_ref=tab.at[lax.rem(z + d, NZ)], dst_ref=tabs.at[IDX[NZ - d]], send_sem=zsend.at[2, d],
            recv_sem=zrecv.at[2, d], device_id=z_id(d), device_id_type=MESH,
        )

    for d in range(1, NZ):
        tabcopy(d).start()
        pending.append(tabcopy(d).wait_send)
    tabs[0] = tab[z]

    qid = iota((SLOTS, SLOTS), 0)

    def queries_of(t):
        return gq[2 * t : 2 * t + 2].reshape(SLOTS, D)

    def pack(t):
        ids = jnp.zeros((GROUPS, 128), jnp.int32)
        order = jnp.zeros((GROUPS, 128), jnp.int32)
        targets = []
        half = GROUPS * (t % 2)
        for o2 in range(2):
            tile = tabs[2 * t + o2].astype(jnp.int32)
            value = tile[half : half + GROUPS]
            ids = ids + jnp.where(value > 0, ((value - 1) & 127) + o2 * QD + 1, 0)
            order = order + jnp.where(value > 0, (value - 1) >> 7, 0)
            targets.append(tile[4:5].astype(F32))
        ids = jnp.concatenate([ids[g : g + 1] for g in range(GROUPS)], axis=1)
        order = jnp.concatenate([order[g : g + 1] for g in range(GROUPS)], axis=1)
        live = ids > 0
        hot = jnp.where(qid == ids - 1, 1.0, 0.0).astype(BF16)
        oht[t] = hot
        pk[t] = dot(hot, queries_of(t), TN).astype(BF16).reshape(PLANE, ROWS, D)
        send(f"rows{t}")
        rb[t, me] = pk[t, me]
        slotinfo[t : t + 1, :] = jnp.where(live, order, -1)
        wanted = jnp.broadcast_to(jnp.concatenate(targets, axis=1), (8, SLOTS)).astype(BF16)
        code = dot(wanted, hot, NN)[0:1, :]
        spread(cmsg, t, jnp.where(live, jnp.where(order == 0, code, -1.0), -2.0))

    def top_scores(t):
        scores = dot(xw[...].reshape(256, D), queries_of(t), NT)
        ts[t] = scores
        largest = jnp.max(scores, axis=0, keepdims=True)
        total = largest + jnp.log(jnp.sum(jnp.exp(scores - largest), axis=0, keepdims=True))
        for o2 in range(2):
            o = ORDER[2 * t + o2]
            tstat[o : o + 1, :] = total[:, o2 * 128 : (o2 + 1) * 128]

    def forward(hop):
        for direction, chunk in flows(hop):
            ag(direction, hop - 1, chunk).wait_recv()
            ag_start(direction, hop, chunk)

    forward(2)
    for d in range(1, NZ):
        tabcopy(d).wait_recv()
    pack(0)
    forward(3)
    pack(1)
    for d in range(1, NX):
        wcopy(d, lax.rem(x - d + NX, NX)).wait_recv()
    top_scores(0)
    forward(4)
    ag(1, 3, 0).wait_recv()
    pack(2)
    for load in loads[6:9]:
        load.wait()
    wext[256:272, :] = jnp.concatenate([mid_ref[...].astype(F32), jnp.zeros((14, D), F32)], axis=0).astype(BF16)
    for g in range(GROUPS):
        cmsg[g, 4:8, :] = jnp.zeros((4, 128), F32)
        gmsg[g, 4:8, :] = jnp.zeros((4, 128), F32)
    top_scores(1)
    ag(0, 3, 1).wait_recv()
    for direction, chunk in flows(4):
        ag(direction, 4, chunk).wait_recv()
    pack(3)
    send("code")
    crecv[me] = cmsg[x // 2]
    top_scores(2)
    top_scores(3)

    def zshare(slot, source, target, d):
        return pltpu.make_async_remote_copy(
            src_ref=source, dst_ref=target.at[d], send_sem=zsend.at[slot, d], recv_sem=zrecv.at[slot, d],
            device_id=z_id(d), device_id_type=MESH,
        )

    def share(slot, source, target):
        for d in range(1, NZ):
            zshare(slot, source, target, d).start()
            pending.append(zshare(slot, source, target, d).wait_send)

    def shared(slot, source, target):
        for d in range(1, NZ):
            zshare(slot, source, target, d).wait_recv()

    def joined(own, views):
        views = [own] + [pltpu.roll(view, NZ - d, axis=0) for d, view in views]
        largest = views[0]
        for view in views[1:]:
            largest = jnp.maximum(largest, view)
        total = jnp.zeros((NZ, 128), F32)
        for view in views:
            total = total + jnp.exp(view - largest)
        return largest + jnp.log(total)

    share(3, tstat, ztop)

    odd = (iota((1, SLOTS), 1) >> 2) & 1

    def holder_scores(s):
        scores = dot(wext[...], rb[s].reshape(SLOTS, D), NT)
        sk[s, 0:LEAF, :] = jnp.where(odd == 0, scores[0:LEAF], scores[LEAF : 2 * LEAF])
        sk[s, LEAF : LEAF + 8, :] = jnp.broadcast_to(
            jnp.where(odd == 0, scores[256:257], scores[257:258]), (8, SLOTS)
        )
        chosen = sk[s, 0:LEAF, :]
        largest = jnp.max(chosen, axis=0, keepdims=True)
        total = largest + jnp.log(jnp.sum(jnp.exp(chosen - largest), axis=0, keepdims=True))
        spread(emsg, 2 * s, total)
        spread(emsg, 2 * s + 1, sk[s, LEAF : LEAF + 1, :])

    for t in range(STEPS):
        arrived(f"rows{t}")
        holder_scores(t)
    send("ex1")
    erecv[me] = emsg[x // 2]
    arrived("code")
    codes = regroup(crecv)
    label_row = iota((LEAF, SLOTS), 0)
    for t in range(STEPS):
        code = codes[t : t + 1, :].astype(jnp.int32)
        spread(gmsg, t, jnp.sum(jnp.where(label_row == code, sk[t, 0:LEAF, :], 0.0), axis=0, keepdims=True))

    shared(3, tstat, ztop)
    zlse[2] = joined(tstat[...], [(d, ztop[d]) for d in range(1, NZ)])

    def query_row(which, t):
        return jnp.concatenate([zlse[which, ORDER[2 * t + o2] : ORDER[2 * t + o2] + 1, :] for o2 in range(2)], axis=1)

    weights = xw[...].reshape(256, D)
    class_row = iota((256, SLOTS), 0)
    grad = jnp.zeros((256, D), F32)
    top_losses = []
    for t in range(STEPS):
        scores = ts[t]
        totals = query_row(2, t)
        target = jnp.concatenate([tabs[2 * t + o2, 5:6, :] for o2 in range(2)], axis=1).astype(jnp.int32)
        here = ((target >> 6) & 7) == z
        place = jnp.where(here, ((target >> 9) << 6) + (target & 63), -1)
        hit = class_row == place
        delta = (jnp.exp(scores - totals) - jnp.where(hit, 1.0, 0.0)).astype(BF16)
        score = jnp.sum(jnp.where(hit, scores, 0.0), axis=0, keepdims=True)
        top_losses.append(jnp.where(here, totals - score, 0.0))
        grad = grad + dot(delta, queries_of(t), NN)
        part[t] = dot(delta, weights, TN)
    core = lax.rem(dp, 2)
    for p in range(PLANE):
        tgs[p % 2, p // 2] = grad[8 * p : 8 * p + 8]
    pair_copy = pltpu.make_async_remote_copy(
        src_ref=tgs.at[1 - core], dst_ref=tgx, send_sem=osend.at[0], recv_sem=orecv.at[0],
        device_id=(dp + 1 - 2 * core, label), device_id_type=MESH,
    )
    pair_copy.start()
    pending.append(pair_copy.wait_send)

    def tg_partner(i):
        return lax.rem(x + i // 4, NX), lax.rem(dp // 2 + i % 4, 4)

    def tg_remote(source, target, i):
        tx, ty = tg_partner(i)
        return pltpu.make_async_remote_copy(
            src_ref=source, dst_ref=target, send_sem=psend.at[12], recv_sem=precv.at[12],
            device_id=(ty * 2 + core, tx * NZ + z), device_id_type=MESH,
        )

    tg_whole = tg_remote(tgr.at[pl.ds(0, 15)], tgr.at[pl.ds(0, 15)], 1)

    arrived("ex1")
    pairs = regroup(erecv)
    number = iota((8, SLOTS), 0)
    loss_rows = []
    for t in range(STEPS):
        mine = slotinfo[t : t + 1, :] == number
        leafs = jnp.where(mine, pairs[2 * t : 2 * t + 1, :], 0.0)
        mids = jnp.where(mine, pairs[2 * t + 1 : 2 * t + 2, :], 0.0)
        pieces = [piece.astype(F32) for piece in split3(leafs) + split3(mids)]
        pieces = pieces + [jnp.where(mine, 1.0, 0.0), jnp.zeros((8, SLOTS), F32)]
        rows = dot(jnp.concatenate(pieces, axis=0).astype(BF16), oht[t], NT)
        there = rows[48:56] > 0.5
        leafs = jnp.where(there, rows[0:8] + rows[8:16] + rows[16:24], NEG)
        mids = jnp.where(there, rows[24:32] + rows[32:40] + rows[40:48], NEG)
        loss_rows.append((there[0:1], mids[0:1]))
        for which, values in enumerate((leafs, mids)):
            largest = jnp.max(values, axis=0, keepdims=True)
            total = largest + jnp.log(jnp.sum(jnp.exp(values - largest), axis=0, keepdims=True))
            for o2 in range(2):
                o = ORDER[2 * t + o2]
                stat[which, o : o + 1, :] = total[:, o2 * 128 : (o2 + 1) * 128]

    share(0, stat, zstat)
    pair_copy.wait_recv()
    own = x * 4 + dp // 2
    tgt[...] = tgs[core] + tgx[...]
    for i in range(1, 16):
        tx, ty = tg_partner(i)
        tg_remote(tgt.at[tx * 4 + ty], tgr.at[own], i).start()
    pending.append(tg_whole.wait_send)
    tgr[own] = tgt[own]
    shared(0, stat, zstat)
    for which in range(2):
        zlse[which] = joined(stat[which], [(d, zstat[d, which]) for d in range(1, NZ)])

    for t in range(STEPS):
        pieces = split3(query_row(0, t)) + split3(query_row(1, t))
        pieces = [piece.astype(F32) for piece in pieces] + [jnp.zeros((10, SLOTS), F32)]
        rows = dot(jnp.concatenate(pieces, axis=0).astype(BF16), oht[t], NN)
        spread(fmsg, 2 * t, rows[0:1] + rows[1:2] + rows[2:3])
        spread(fmsg, 2 * t + 1, rows[3:4] + rows[4:5] + rows[5:6])
    send("ex2")
    frecv[me] = fmsg[x // 2]
    send("goal")
    grecv[me] = gmsg[x // 2]

    def losscopy(o):
        return pltpu.make_async_remote_copy(
            src_ref=losss.at[o], dst_ref=lossr.at[o], send_sem=zsend.at[1, o],
            recv_sem=zrecv.at[1, o], device_id=z_id(o), device_id_type=MESH,
        )

    arrived("ex2")
    scalars = regroup(frecv)
    even = odd == 0
    deltas = [None] * STEPS

    def back_rows(t):
        code = codes[t : t + 1, :].astype(jnp.int32)
        live = code > -2
        hit = jnp.where(label_row == code, 1.0, 0.0)
        delta = jnp.where(live, jnp.exp(sk[t, 0:LEAF, :] - scalars[2 * t : 2 * t + 1, :]) - hit, 0.0)
        middle = jnp.exp(sk[t, LEAF : LEAF + 1, :] - scalars[2 * t + 1 : 2 * t + 2, :])
        middle = jnp.where(live, middle - jnp.where(code >= 0, 1.0, 0.0), 0.0)
        full = jnp.concatenate(
            [
                jnp.where(even, delta, 0.0), jnp.where(even, 0.0, delta),
                jnp.where(even, middle, 0.0), jnp.where(even, 0.0, middle),
                jnp.zeros((14, SLOTS), F32),
            ],
            axis=0,
        ).astype(BF16)
        deltas[t] = full
        ob[t] = dot(full, wext[...], TN).astype(BF16).reshape(PLANE, ROWS, D)

    def send_back(t):
        send(f"ret{t}")
        pbk[t, me] = ob[t, me]

    for t in (3, 2, 1, 0):
        back_rows(t)
        send_back(t)

    tg_whole.wait_recv()
    tg_sum = tgr[0]
    for f in range(1, PLANE // 2):
        tg_sum = tg_sum + tgr[f]
    tg_ref[pl.ds(pl.multiple_of(dp * 8, 8), 8), :] = tg_sum

    def tgcopy(d, who):
        rows = pl.ds(pl.multiple_of(who * 8, 8), 8)
        return pltpu.make_async_remote_copy(
            src_ref=tg_ref.at[rows], dst_ref=tg_ref.at[rows], send_sem=osend.at[d],
            recv_sem=orecv.at[d], device_id=dp_id(d), device_id_type=MESH,
        )

    for d in range(1, NDP):
        tgcopy(d, dp).start()
        pending.append(tgcopy(d, dp).wait_send)

    def send_losses():
        arrived("goal")
        goals = regroup(grecv)
        for t in range(STEPS):
            goal = jnp.where(slotinfo[t : t + 1, :] == 0, goals[t : t + 1, :], 0.0)
            pieces = [piece.astype(F32) for piece in split3(goal)] + [jnp.zeros((13, SLOTS), F32)]
            rows = dot(jnp.concatenate(pieces, axis=0).astype(BF16), oht[t], NT)
            first, middle = loss_rows[t]
            leaf_query = jnp.where(first, query_row(0, t) - (rows[0:1] + rows[1:2] + rows[2:3]), 0.0)
            mid_query = jnp.where(first, query_row(1, t) - middle, 0.0)
            for o2 in range(2):
                o = ORDER[2 * t + o2]
                span = slice(o2 * 128, (o2 + 1) * 128)
                losss[o] = jnp.concatenate(
                    [top_losses[t][:, span], mid_query[:, span], leaf_query[:, span], jnp.zeros((5, 128), F32)],
                    axis=0,
                )
        for o in range(1, NZ):
            losscopy(o).start()
            pending.append(losscopy(o).wait_send)


    def store(n, source, target):
        copy = pltpu.make_async_copy(source, target, outsem.at[n])
        copy.start()
        pending.append(copy.wait)

    halves = (pl.ds(0, 64), pl.ds(64, 64))

    def rs(direction, hop, chunk):
        return pltpu.make_async_remote_copy(
            src_ref=rsS.at[direction, hop, halves[chunk]],
            dst_ref=rsR.at[direction, hop, halves[chunk]],
            send_sem=rssend.at[direction, hop, chunk], recv_sem=rsrecv.at[direction, hop, chunk],
            device_id=z_id(1 if direction == 0 else NZ - 1), device_id_type=MESH,
        )

    def rs_step(direction, hop, chunk):
        o = 4 - hop if direction == 0 else 4 + hop
        index = IDX[o]
        rows = pl.ds((index % 2) * QD + chunk * 64, 64)
        value = part[index // 2, rows, :]
        if hop > 1 or (hop == 1 and chunk == direction):
            rs(direction, hop - 1, chunk).wait_recv()
            value = value + rsR[direction, hop - 1, halves[chunk], :].astype(F32)
        rsS[direction, hop, halves[chunk], :] = value.astype(BF16)
        rs(direction, hop, chunk).start()
        pending.append(rs(direction, hop, chunk).wait_send)

    def returned(t):
        arrived(f"ret{t}")
        part[t] = part[t] + dot(oht[t], pbk[t].reshape(SLOTS, D), NN)

    send_losses()
    returned(3)
    rs_step(0, 0, 0)
    rs_step(1, 0, 1)
    rs_step(1, 1, 0)
    grads = jnp.zeros((272, D), F32)
    for t in range(STEPS):
        grads = grads + dot(deltas[t], rb[t].reshape(SLOTS, D), NN)
    lg_ref[...] = grads[0:256].reshape(2, LEAF, D)
    mg_ref[...] = grads[256:258]
    store(0, lg_ref, lg_out)
    store(1, mg_ref, mg_out)
    returned(2)
    rs_step(0, 1, 1)
    rs_step(1, 1, 1)
    rs_step(0, 1, 0)
    rs_step(1, 2, 0)
    rs_step(1, 2, 1)
    returned(1)
    rs_step(0, 2, 1)
    rs_step(1, 3, 0)
    rs_step(0, 2, 0)
    rs_step(1, 3, 1)
    returned(0)
    rs_step(0, 3, 1)
    rs_step(0, 3, 0)

    for d in range(1, NDP):
        tgcopy(d, lax.rem(dp - d + NDP, NDP)).wait_recv()
    store(2, tg_ref, tg_out)
    for o in range(1, NZ):
        losscopy(o).wait_recv()
    losses = losss[0]
    for o in range(1, NZ):
        losses = losses + lossr[o]
    loss_ref[...] = losses[0:3]
    store(3, loss_ref, loss_out)
    for chunk in (0, 1):
        rs(1, 3, chunk).wait_recv()
    for chunk in (1, 0):
        rs(0, 3, chunk).wait_recv()
    qg_ref[...] = part[0, 0:QD, :] + rsR[0, 3].astype(F32) + rsR[1, 3].astype(F32)
    store(4, qg_ref, qg_out)
    finish()


def place_outputs(*refs):
    for source, target in zip(refs[0:5], refs[5:10]):
        target[...] = source[...]


def per_device(queries, shortlist, slab_slot, top_target, leaf_target, top_weight, mid_weight, leaf_weight):
    hbm = pl.BlockSpec(memory_space=pltpu.HBM)
    vmem = pl.BlockSpec(memory_space=pltpu.VMEM)
    sem = pltpu.SemaphoreType.DMA
    results = (
        jax.ShapeDtypeStruct((QD, D), F32),
        jax.ShapeDtypeStruct((64, D), F32),
        jax.ShapeDtypeStruct((2, D), F32),
        jax.ShapeDtypeStruct((2, LEAF, D), F32),
        jax.ShapeDtypeStruct((3, QD), F32),
    )
    scratch = [
        pltpu.VMEM((NZ, QD, D), BF16),
        pltpu.VMEM((SHORT, QD), jnp.int32),
        pltpu.VMEM((1, BLOCKS), jnp.int32),
        pltpu.VMEM((1, QD), jnp.int32),
        pltpu.VMEM((1, QD), jnp.int32),
        pltpu.VMEM((2, D), BF16),
        pltpu.VMEM((NZ, 8, 128), F32),
        pltpu.VMEM((NZ, 8, 128), F32),
        pltpu.VMEM((NX, 64, D), BF16),
        pltpu.VMEM((272, D), BF16),
        pltpu.VMEM((STEPS, SLOTS, SLOTS), BF16),
        pltpu.VMEM((8, SLOTS), jnp.int32),
        pltpu.VMEM((STEPS, PLANE, ROWS, D), BF16),
        pltpu.VMEM((STEPS, PLANE, ROWS, D), BF16),
        pltpu.VMEM((STEPS, LEAF + 8, SLOTS), F32),
        pltpu.VMEM((STEPS, 256, SLOTS), F32),
        pltpu.VMEM((GROUPS, 8, 128), F32),
        pltpu.VMEM((PLANE, 8, 128), F32),
        pltpu.VMEM((GROUPS, 8, 128), F32),
        pltpu.VMEM((PLANE, 8, 128), F32),
        pltpu.VMEM((GROUPS, 8, 128), F32),
        pltpu.VMEM((PLANE, 8, 128), F32),
        pltpu.VMEM((GROUPS, 8, 128), F32),
        pltpu.VMEM((PLANE, 8, 128), F32),
        pltpu.VMEM((2, NZ, 128), F32),
        pltpu.VMEM((NZ, 2, NZ, 128), F32),
        pltpu.VMEM((3, NZ, 128), F32),
        pltpu.VMEM((NZ, 128), F32),
        pltpu.VMEM((NZ, NZ, 128), F32),
        pltpu.VMEM((STEPS, SLOTS, D), F32),
        pltpu.VMEM((STEPS, PLANE, ROWS, D), BF16),
        pltpu.VMEM((STEPS, PLANE, ROWS, D), BF16),
        pltpu.VMEM((2, PLANE // 2, 8, D), F32),
        pltpu.VMEM((PLANE // 2, 8, D), F32),
        pltpu.VMEM((PLANE // 2, 8, D), F32),
        pltpu.VMEM((PLANE // 2, 8, D), F32),
        pltpu.VMEM((NZ, 8, 128), F32),
        pltpu.VMEM((NZ, 8, 128), F32),
        pltpu.VMEM((2, 4, QD, D), BF16),
        pltpu.VMEM((2, 4, QD, D), BF16),
        *[pltpu.VMEM(result.shape, F32) for result in results],
        sem((13,)), sem((13,)),
        sem((2, 4, 4)), sem((2, 4, 4)),
        sem((2, 4, 2)), sem((2, 4, 2)),
        sem((4, NZ)), sem((4, NZ)),
        sem((NX,)), sem((NX,)),
        sem((NDP,)), sem((NDP,)),
        sem((9,)), sem((5,)),
    ]
    arrays = pl.pallas_call(
        kernel,
        out_shape=results,
        in_specs=[hbm] * 8,
        out_specs=(hbm,) * 5,
        scratch_shapes=scratch,
        compiler_params=pltpu.CompilerParams(
            collective_id=0, has_side_effects=True, vmem_limit_bytes=60 << 20
        ),
    )(
        queries, shortlist.T, slab_slot.reshape(1, -1), top_target.reshape(1, -1), leaf_target.reshape(1, -1),
        leaf_weight, mid_weight, top_weight,
    )
    return pl.pallas_call(
        place_outputs,
        out_shape=results,
        in_specs=[vmem] * 5,
        out_specs=(vmem,) * 5,
        compiler_params=pltpu.CompilerParams(vmem_limit_bytes=60 << 20),
    )(*arrays)


def solution(mesh):
    both = ("dp", "label")
    in_specs = (
        P(both, None), P(both, None), P(), P(both), P(both),
        P("label", None), P(both, None), P(both, None, None),
    )
    out_specs = (
        P(both, None), P("label", None), P(both, None), P(both, None, None), P(None, both),
    )
    return jax.shard_map(
        per_device, mesh=mesh, in_specs=in_specs, out_specs=out_specs, check_vma=False
    )
```

```python
import jax
import jax.numpy as jnp
from jax import lax
from jax.experimental import pallas as pl
from jax.experimental.pallas import tpu as pltpu
from jax.sharding import PartitionSpec as P

D = 512
BLOCKS = 512
QD = 128
SHORT = 4
LEAF = 128
NZ = 8
NX = 4
NDP = 8
PLANE = NX * NDP
STEPS = 4
ROWS = 8
SLOTS = PLANE * ROWS
GROUPS = 2
ORDER = (0, 1, 7, 2, 6, 3, 5, 4)
IDX = tuple(ORDER.index(o) for o in range(NZ))
NEG = -1e30
FAR_PLANE = sorted(range(1, PLANE), key=lambda i: -min(i // NDP, NX - i // NDP) - min(i % NDP, NDP - i % NDP) / 2)
FAR_Z = (4, 3, 5, 2, 6, 1, 7)
MESH = pl.DeviceIdType.MESH
F32 = jnp.float32
BF16 = jnp.bfloat16
NT = (((1,), (1,)), ((), ()))
TN = (((0,), (0,)), ((), ()))
NN = (((1,), (0,)), ((), ()))


def dot(a, b, dims):
    return lax.dot_general(a, b, dims, preferred_element_type=F32)


def split3(v):
    hi = v.astype(BF16)
    rest = v - hi.astype(F32)
    mid = rest.astype(BF16)
    low = (rest - mid.astype(F32)).astype(BF16)
    return hi, mid, low


def iota(shape, dim):
    return lax.broadcasted_iota(jnp.int32, shape, dim)


def kernel(
    query_in, short_in, slab_in, target_in, leaftarget_in, leaf_in, mid_in, topw_in,
    qg_out, tg_out, mg_out, lg_out, loss_out,
    gq, short_ref, slab_ref, target_ref, leaftarget_ref, mid_ref, tab, tabs,
    xw, wext, oht, slotinfo, pk, rb, sk, ts, cmsg, crecv, emsg, erecv, gmsg, grecv, fmsg, frecv,
    stat, zstat, zlse, tstat, ztop, part, ob, pbk, tgs, tgx, tgt, tgr, losss, lossr, rsS, rsR,
    qg_ref, tg_ref, mg_ref, lg_ref, loss_ref,
    psend, precv, agsend, agrecv, rssend, rsrecv, zsend, zrecv, wsend, wrecv, osend, orecv, insem, outsem,
):
    dp = lax.axis_index("dp")
    label = lax.axis_index("label")
    x = label // NZ
    z = lax.rem(label, NZ)
    me = x * NDP + dp

    def partner(i):
        tx, td = lax.rem(x + i // NDP, NX), lax.rem(dp + i % NDP, NDP)
        return tx, td

    def plane_id(i):
        tx, td = partner(i)
        return (td, tx * NZ + z)

    def z_id(d):
        return (dp, x * NZ + lax.rem(z + d, NZ))

    def x_id(d):
        return (dp, lax.rem(x + d, NX) * NZ + z)

    def dp_id(d):
        return (lax.rem(dp + d, NDP), label)

    pending = []

    def finish():
        for wait in pending:
            wait()

    barrier = pltpu.get_barrier_semaphore()
    for i in range(1, PLANE):
        pl.semaphore_signal(barrier, inc=1, device_id=plane_id(i), device_id_type=MESH)
    for d in range(1, NZ):
        pl.semaphore_signal(barrier, inc=1, device_id=z_id(d), device_id_type=MESH)

    loads = [
        pltpu.make_async_copy(a, b, insem.at[n])
        for n, (a, b) in enumerate((
            (query_in, gq.at[0]), (short_in, short_ref), (slab_in, slab_ref), (target_in, target_ref),
            (leaftarget_in, leaftarget_ref), (topw_in, xw.at[x]), (mid_in, mid_ref),
            (leaf_in.at[0], wext.at[pl.ds(0, LEAF)]), (leaf_in.at[1], wext.at[pl.ds(LEAF, LEAF)]),
        ))
    ]
    for load in loads:
        load.start()
    loads[0].wait()
    loads[5].wait()
    pl.semaphore_wait(barrier, PLANE - 1 + NZ - 1)

    cuts = ((0, 64), (64, 64))

    def ag(direction, hop, chunk):
        start, length = cuts[chunk]
        if direction == 0:
            src, dst, to = IDX[(NZ - hop + 1) % NZ], IDX[NZ - hop], 1
        else:
            src, dst, to = IDX[hop - 1], IDX[hop], NZ - 1
        rows = pl.ds(start, length)
        return pltpu.make_async_remote_copy(
            src_ref=gq.at[src, rows], dst_ref=gq.at[dst, rows],
            send_sem=agsend.at[direction, hop - 1, chunk],
            recv_sem=agrecv.at[direction, hop - 1, chunk],
            device_id=z_id(to), device_id_type=MESH,
        )

    def ag_start(direction, hop, chunk):
        copy = ag(direction, hop, chunk)
        copy.start()
        pending.append(copy.wait_send)

    def flows(hop):
        return [(0, 0), (1, 1), (0, 1), (1, 0)] if hop < 4 else [(0, 0), (1, 1)]

    for direction, chunk in flows(1):
        ag_start(direction, 1, chunk)

    def wcopy(d, owner):
        return pltpu.make_async_remote_copy(
            src_ref=xw.at[owner], dst_ref=xw.at[owner], send_sem=wsend.at[d], recv_sem=wrecv.at[d],
            device_id=x_id(d), device_id_type=MESH,
        )

    for d in range(1, NX):
        wcopy(d, x).start()
        pending.append(wcopy(d, x).wait_send)

    def remote(phase, source, target, to):
        return pltpu.make_async_remote_copy(
            src_ref=source, dst_ref=target, send_sem=psend.at[phase], recv_sem=precv.at[phase],
            device_id=to, device_id_type=MESH,
        )

    span31 = pl.ds(0, PLANE - 1)
    exchanges = {
        "code": (8, lambda tx, td: cmsg.at[tx // 2], crecv),
        "ex1": (9, lambda tx, td: emsg.at[tx // 2], erecv),
        "goal": (10, lambda tx, td: gmsg.at[tx // 2], grecv),
        "ex2": (11, lambda tx, td: fmsg.at[tx // 2], frecv),
    }
    for t in range(STEPS):
        exchanges[f"rows{t}"] = (t, lambda tx, td, t=t: pk.at[t, tx * NDP + td], rb.at[t])
        exchanges[f"ret{t}"] = (4 + t, lambda tx, td, t=t: ob.at[t, tx * NDP + td], pbk.at[t])

    def whole(name):
        phase, _, target = exchanges[name]
        return remote(phase, target.at[span31], target.at[span31], plane_id(1))

    def send(name):
        phase, source, target = exchanges[name]
        for i in FAR_PLANE:
            remote(phase, source(*partner(i)), target.at[me], plane_id(i)).start()
        pending.append(whole(name).wait_send)

    def arrived(name):
        whole(name).wait_recv()

    lane = iota((8, 128), 1)

    def regroup(received):
        mine = lax.rem(x, 2) * NDP + dp
        groups = []
        for g in range(GROUPS):
            out = jnp.zeros((8, 128), F32)
            for j in range(16):
                turned = pltpu.roll(received[g * 16 + j], lax.rem(j - mine + 16, 16) * ROWS, axis=1)
                out = jnp.where(lane // ROWS == j, turned, out)
            groups.append(out)
        return jnp.concatenate(groups, axis=1)

    def spread(message, row, value):
        for g in range(GROUPS):
            message[g, row : row + 1, :] = value[:, g * 128 : (g + 1) * 128]

    for load in loads[1:5]:
        load.wait()
    wide = iota((QD, BLOCKS), 1)
    narrow = iota((QD, QD), 1)
    query_col = iota((QD, 1), 0)
    eye = iota((QD, QD), 0) == narrow
    slab = slab_ref[...].astype(F32)
    lower = jnp.where(iota((QD, QD), 1) < iota((QD, QD), 0), 1.0, 0.0).astype(BF16)
    base = jnp.zeros((1, BLOCKS), F32)
    table = jnp.zeros((QD, QD), F32)
    for j in range(SHORT):
        named = jnp.sum(jnp.where(eye, short_ref[j : j + 1, :].astype(F32), 0.0), axis=1, keepdims=True).astype(jnp.int32)
        position = jnp.sum(jnp.where(wide == named, slab, 0.0), axis=1, keepdims=True).astype(jnp.int32)
        taken = wide == position
        ones = jnp.where(taken, 1.0, 0.0)
        before = dot(lower, ones.astype(BF16), NN) + base
        base = base + jnp.sum(ones, axis=0, keepdims=True)
        rank = jnp.sum(jnp.where(taken, before, 0.0), axis=1, keepdims=True).astype(jnp.int32)
        holder = position >> 1
        holder_z, holder_x, holder_dp = holder & 7, (holder >> 3) & 3, holder >> 5
        offset = (z - holder_z + NZ) & 7
        index = jnp.zeros((QD, 1), jnp.int32)
        for o in range(NZ):
            index = jnp.where(offset == o, IDX[o], index)
        holder = holder_x * NDP + holder_dp
        place = (holder & 15) * ROWS + (position & 1) * 4 + (index & 1) * 2 + rank
        row = holder_z * 4 + ((index >> 1) & 1) * GROUPS + (holder >> 4)
        left = jnp.where(narrow == row, (query_col + 1).astype(F32), jnp.where(narrow == row + 32, j * 128.0, 0.0))
        right = jnp.where(narrow == place, 1.0, 0.0)
        table = table + dot(left.astype(BF16), right.astype(BF16), TN)
    table = table[0:32] + table[32:64]
    for p in range(NZ):
        tab[p, 0:4, :] = table[4 * p : 4 * p + 4]
        tab[p, 4:5, :] = leaftarget_ref[...].astype(F32)
        tab[p, 5:6, :] = target_ref[...].astype(F32)
        tab[p, 6:8, :] = jnp.zeros((2, 128), F32)

    def tabcopy(d):
        return pltpu.make_async_remote_copy(
            src_ref=tab.at[lax.rem(z + d, NZ)], dst_ref=tabs.at[IDX[NZ - d]], send_sem=zsend.at[2, d],
            recv_sem=zrecv.at[2, d], device_id=z_id(d), device_id_type=MESH,
        )

    for d in range(1, NZ):
        tabcopy(d).start()
        pending.append(tabcopy(d).wait_send)
    tabs[0] = tab[z]

    qid = iota((SLOTS, SLOTS), 0)

    def queries_of(t):
        return gq[2 * t : 2 * t + 2].reshape(SLOTS, D)

    def pack(t):
        ids = jnp.zeros((GROUPS, 128), jnp.int32)
        order = jnp.zeros((GROUPS, 128), jnp.int32)
        targets = []
        half = GROUPS * (t % 2)
        for o2 in range(2):
            tile = tabs[2 * t + o2].astype(jnp.int32)
            value = tile[half : half + GROUPS]
            ids = ids + jnp.where(value > 0, ((value - 1) & 127) + o2 * QD + 1, 0)
            order = order + jnp.where(value > 0, (value - 1) >> 7, 0)
            targets.append(tile[4:5].astype(F32))
        ids = jnp.concatenate([ids[g : g + 1] for g in range(GROUPS)], axis=1)
        order = jnp.concatenate([order[g : g + 1] for g in range(GROUPS)], axis=1)
        live = ids > 0
        hot = jnp.where(qid == ids - 1, 1.0, 0.0).astype(BF16)
        oht[t] = hot
        pk[t] = dot(hot, queries_of(t), TN).astype(BF16).reshape(PLANE, ROWS, D)
        send(f"rows{t}")
        rb[t, me] = pk[t, me]
        slotinfo[t : t + 1, :] = jnp.where(live, order, -1)
        wanted = jnp.broadcast_to(jnp.concatenate(targets, axis=1), (8, SLOTS)).astype(BF16)
        code = dot(wanted, hot, NN)[0:1, :]
        spread(cmsg, t, jnp.where(live, jnp.where(order == 0, code, -1.0), -2.0))

    def top_scores(t):
        scores = dot(xw[...].reshape(256, D), queries_of(t), NT)
        ts[t] = scores
        largest = jnp.max(scores, axis=0, keepdims=True)
        total = largest + jnp.log(jnp.sum(jnp.exp(scores - largest), axis=0, keepdims=True))
        for o2 in range(2):
            o = ORDER[2 * t + o2]
            tstat[o : o + 1, :] = total[:, o2 * 128 : (o2 + 1) * 128]

    def forward(hop):
        for direction, chunk in flows(hop):
            ag(direction, hop - 1, chunk).wait_recv()
            ag_start(direction, hop, chunk)

    forward(2)
    for d in range(1, NZ):
        tabcopy(d).wait_recv()
    pack(0)
    forward(3)
    pack(1)
    for d in range(1, NX):
        wcopy(d, lax.rem(x - d + NX, NX)).wait_recv()
    top_scores(0)
    forward(4)
    ag(1, 3, 0).wait_recv()
    pack(2)
    for load in loads[6:9]:
        load.wait()
    wext[256:272, :] = jnp.concatenate([mid_ref[...].astype(F32), jnp.zeros((14, D), F32)], axis=0).astype(BF16)
    for g in range(GROUPS):
        cmsg[g, 4:8, :] = jnp.zeros((4, 128), F32)
        gmsg[g, 4:8, :] = jnp.zeros((4, 128), F32)
    top_scores(1)
    ag(0, 3, 1).wait_recv()
    for direction, chunk in flows(4):
        ag(direction, 4, chunk).wait_recv()
    pack(3)
    send("code")
    crecv[me] = cmsg[x // 2]
    top_scores(2)
    top_scores(3)

    def zshare(slot, source, target, d):
        return pltpu.make_async_remote_copy(
            src_ref=source, dst_ref=target.at[d], send_sem=zsend.at[slot, d], recv_sem=zrecv.at[slot, d],
            device_id=z_id(d), device_id_type=MESH,
        )

    def share(slot, source, target):
        for d in FAR_Z:
            zshare(slot, source, target, d).start()
            pending.append(zshare(slot, source, target, d).wait_send)

    def shared(slot, source, target):
        for d in range(1, NZ):
            zshare(slot, source, target, d).wait_recv()

    def joined(own, views):
        views = [own] + [pltpu.roll(view, NZ - d, axis=0) for d, view in views]
        largest = views[0]
        for view in views[1:]:
            largest = jnp.maximum(largest, view)
        total = jnp.zeros((NZ, 128), F32)
        for view in views:
            total = total + jnp.exp(view - largest)
        return largest + jnp.log(total)

    share(3, tstat, ztop)

    odd = (iota((1, SLOTS), 1) >> 2) & 1

    def holder_scores(s):
        scores = dot(wext[...], rb[s].reshape(SLOTS, D), NT)
        sk[s, 0:LEAF, :] = jnp.where(odd == 0, scores[0:LEAF], scores[LEAF : 2 * LEAF])
        sk[s, LEAF : LEAF + 8, :] = jnp.broadcast_to(
            jnp.where(odd == 0, scores[256:257], scores[257:258]), (8, SLOTS)
        )
        chosen = sk[s, 0:LEAF, :]
        largest = jnp.max(chosen, axis=0, keepdims=True)
        total = largest + jnp.log(jnp.sum(jnp.exp(chosen - largest), axis=0, keepdims=True))
        spread(emsg, 2 * s, total)
        spread(emsg, 2 * s + 1, sk[s, LEAF : LEAF + 1, :])

    for t in range(STEPS):
        arrived(f"rows{t}")
        holder_scores(t)
    send("ex1")
    erecv[me] = emsg[x // 2]
    arrived("code")
    codes = regroup(crecv)
    label_row = iota((LEAF, SLOTS), 0)
    for t in range(STEPS):
        code = codes[t : t + 1, :].astype(jnp.int32)
        spread(gmsg, t, jnp.sum(jnp.where(label_row == code, sk[t, 0:LEAF, :], 0.0), axis=0, keepdims=True))

    shared(3, tstat, ztop)
    zlse[2] = joined(tstat[...], [(d, ztop[d]) for d in range(1, NZ)])

    def query_row(which, t):
        return jnp.concatenate([zlse[which, ORDER[2 * t + o2] : ORDER[2 * t + o2] + 1, :] for o2 in range(2)], axis=1)

    weights = xw[...].reshape(256, D)
    class_row = iota((256, SLOTS), 0)
    grad = jnp.zeros((256, D), F32)
    top_losses = []
    for t in range(STEPS):
        scores = ts[t]
        totals = query_row(2, t)
        target = jnp.concatenate([tabs[2 * t + o2, 5:6, :] for o2 in range(2)], axis=1).astype(jnp.int32)
        here = ((target >> 6) & 7) == z
        place = jnp.where(here, ((target >> 9) << 6) + (target & 63), -1)
        hit = class_row == place
        delta = (jnp.exp(scores - totals) - jnp.where(hit, 1.0, 0.0)).astype(BF16)
        score = jnp.sum(jnp.where(hit, scores, 0.0), axis=0, keepdims=True)
        top_losses.append(jnp.where(here, totals - score, 0.0))
        grad = grad + dot(delta, queries_of(t), NN)
        part[t] = dot(delta, weights, TN)
    core = lax.rem(dp, 2)
    for p in range(PLANE):
        tgs[p % 2, p // 2] = grad[8 * p : 8 * p + 8]
    pair_copy = pltpu.make_async_remote_copy(
        src_ref=tgs.at[1 - core], dst_ref=tgx, send_sem=osend.at[0], recv_sem=orecv.at[0],
        device_id=(dp + 1 - 2 * core, label), device_id_type=MESH,
    )
    pair_copy.start()
    pending.append(pair_copy.wait_send)

    def tg_partner(i):
        return lax.rem(x + i // 4, NX), lax.rem(dp // 2 + i % 4, 4)

    def tg_remote(source, target, i):
        tx, ty = tg_partner(i)
        return pltpu.make_async_remote_copy(
            src_ref=source, dst_ref=target, send_sem=psend.at[12], recv_sem=precv.at[12],
            device_id=(ty * 2 + core, tx * NZ + z), device_id_type=MESH,
        )

    tg_whole = tg_remote(tgr.at[pl.ds(0, 15)], tgr.at[pl.ds(0, 15)], 1)

    arrived("ex1")
    pairs = regroup(erecv)
    number = iota((8, SLOTS), 0)
    loss_rows = []
    for t in range(STEPS):
        mine = slotinfo[t : t + 1, :] == number
        leafs = jnp.where(mine, pairs[2 * t : 2 * t + 1, :], 0.0)
        mids = jnp.where(mine, pairs[2 * t + 1 : 2 * t + 2, :], 0.0)
        pieces = [piece.astype(F32) for piece in split3(leafs) + split3(mids)]
        pieces = pieces + [jnp.where(mine, 1.0, 0.0), jnp.zeros((8, SLOTS), F32)]
        rows = dot(jnp.concatenate(pieces, axis=0).astype(BF16), oht[t], NT)
        there = rows[48:56] > 0.5
        leafs = jnp.where(there, rows[0:8] + rows[8:16] + rows[16:24], NEG)
        mids = jnp.where(there, rows[24:32] + rows[32:40] + rows[40:48], NEG)
        loss_rows.append((there[0:1], mids[0:1]))
        for which, values in enumerate((leafs, mids)):
            largest = jnp.max(values, axis=0, keepdims=True)
            total = largest + jnp.log(jnp.sum(jnp.exp(values - largest), axis=0, keepdims=True))
            for o2 in range(2):
                o = ORDER[2 * t + o2]
                stat[which, o : o + 1, :] = total[:, o2 * 128 : (o2 + 1) * 128]

    share(0, stat, zstat)
    pair_copy.wait_recv()
    own = x * 4 + dp // 2
    tgt[...] = tgs[core] + tgx[...]
    for i in range(1, 16):
        tx, ty = tg_partner(i)
        tg_remote(tgt.at[tx * 4 + ty], tgr.at[own], i).start()
    pending.append(tg_whole.wait_send)
    tgr[own] = tgt[own]
    shared(0, stat, zstat)
    for which in range(2):
        zlse[which] = joined(stat[which], [(d, zstat[d, which]) for d in range(1, NZ)])

    for t in range(STEPS):
        pieces = split3(query_row(0, t)) + split3(query_row(1, t))
        pieces = [piece.astype(F32) for piece in pieces] + [jnp.zeros((10, SLOTS), F32)]
        rows = dot(jnp.concatenate(pieces, axis=0).astype(BF16), oht[t], NN)
        spread(fmsg, 2 * t, rows[0:1] + rows[1:2] + rows[2:3])
        spread(fmsg, 2 * t + 1, rows[3:4] + rows[4:5] + rows[5:6])
    send("ex2")
    frecv[me] = fmsg[x // 2]
    send("goal")
    grecv[me] = gmsg[x // 2]

    def losscopy(o):
        return pltpu.make_async_remote_copy(
            src_ref=losss.at[o], dst_ref=lossr.at[o], send_sem=zsend.at[1, o],
            recv_sem=zrecv.at[1, o], device_id=z_id(o), device_id_type=MESH,
        )

    arrived("ex2")
    scalars = regroup(frecv)
    even = odd == 0
    deltas = [None] * STEPS

    def back_rows(t):
        code = codes[t : t + 1, :].astype(jnp.int32)
        live = code > -2
        hit = jnp.where(label_row == code, 1.0, 0.0)
        delta = jnp.where(live, jnp.exp(sk[t, 0:LEAF, :] - scalars[2 * t : 2 * t + 1, :]) - hit, 0.0)
        middle = jnp.exp(sk[t, LEAF : LEAF + 1, :] - scalars[2 * t + 1 : 2 * t + 2, :])
        middle = jnp.where(live, middle - jnp.where(code >= 0, 1.0, 0.0), 0.0)
        full = jnp.concatenate(
            [
                jnp.where(even, delta, 0.0), jnp.where(even, 0.0, delta),
                jnp.where(even, middle, 0.0), jnp.where(even, 0.0, middle),
                jnp.zeros((14, SLOTS), F32),
            ],
            axis=0,
        ).astype(BF16)
        deltas[t] = full
        ob[t] = dot(full, wext[...], TN).astype(BF16).reshape(PLANE, ROWS, D)

    def send_back(t):
        send(f"ret{t}")
        pbk[t, me] = ob[t, me]

    for t in (3, 2, 1, 0):
        back_rows(t)
        send_back(t)

    tg_whole.wait_recv()
    tg_sum = tgr[0]
    for f in range(1, PLANE // 2):
        tg_sum = tg_sum + tgr[f]
    tg_ref[pl.ds(pl.multiple_of(dp * 8, 8), 8), :] = tg_sum

    def tgcopy(d, who):
        rows = pl.ds(pl.multiple_of(who * 8, 8), 8)
        return pltpu.make_async_remote_copy(
            src_ref=tg_ref.at[rows], dst_ref=tg_ref.at[rows], send_sem=osend.at[d],
            recv_sem=orecv.at[d], device_id=dp_id(d), device_id_type=MESH,
        )

    for d in range(1, NDP):
        tgcopy(d, dp).start()
        pending.append(tgcopy(d, dp).wait_send)

    def send_losses():
        arrived("goal")
        goals = regroup(grecv)
        for t in range(STEPS):
            goal = jnp.where(slotinfo[t : t + 1, :] == 0, goals[t : t + 1, :], 0.0)
            pieces = [piece.astype(F32) for piece in split3(goal)] + [jnp.zeros((13, SLOTS), F32)]
            rows = dot(jnp.concatenate(pieces, axis=0).astype(BF16), oht[t], NT)
            first, middle = loss_rows[t]
            leaf_query = jnp.where(first, query_row(0, t) - (rows[0:1] + rows[1:2] + rows[2:3]), 0.0)
            mid_query = jnp.where(first, query_row(1, t) - middle, 0.0)
            for o2 in range(2):
                o = ORDER[2 * t + o2]
                span = slice(o2 * 128, (o2 + 1) * 128)
                losss[o] = jnp.concatenate(
                    [top_losses[t][:, span], mid_query[:, span], leaf_query[:, span], jnp.zeros((5, 128), F32)],
                    axis=0,
                )
        for o in range(1, NZ):
            losscopy(o).start()
            pending.append(losscopy(o).wait_send)


    def store(n, source, target):
        copy = pltpu.make_async_copy(source, target, outsem.at[n])
        copy.start()
        pending.append(copy.wait)

    halves = (pl.ds(0, 64), pl.ds(64, 64))

    def rs(direction, hop, chunk):
        return pltpu.make_async_remote_copy(
            src_ref=rsS.at[direction, hop, halves[chunk]],
            dst_ref=rsR.at[direction, hop, halves[chunk]],
            send_sem=rssend.at[direction, hop, chunk], recv_sem=rsrecv.at[direction, hop, chunk],
            device_id=z_id(1 if direction == 0 else NZ - 1), device_id_type=MESH,
        )

    def rs_step(direction, hop, chunk):
        o = 4 - hop if direction == 0 else 4 + hop
        index = IDX[o]
        rows = pl.ds((index % 2) * QD + chunk * 64, 64)
        value = part[index // 2, rows, :]
        if hop > 1 or (hop == 1 and chunk == direction):
            rs(direction, hop - 1, chunk).wait_recv()
            value = value + rsR[direction, hop - 1, halves[chunk], :].astype(F32)
        rsS[direction, hop, halves[chunk], :] = value.astype(BF16)
        rs(direction, hop, chunk).start()
        pending.append(rs(direction, hop, chunk).wait_send)

    def returned(t):
        arrived(f"ret{t}")
        part[t] = part[t] + dot(oht[t], pbk[t].reshape(SLOTS, D), NN)

    send_losses()
    returned(3)
    rs_step(0, 0, 0)
    rs_step(1, 0, 1)
    rs_step(1, 1, 0)
    grads = jnp.zeros((272, D), F32)
    for t in range(STEPS):
        grads = grads + dot(deltas[t], rb[t].reshape(SLOTS, D), NN)
    lg_ref[...] = grads[0:256].reshape(2, LEAF, D)
    mg_ref[...] = grads[256:258]
    store(0, lg_ref, lg_out)
    store(1, mg_ref, mg_out)
    returned(2)
    rs_step(0, 1, 1)
    rs_step(1, 1, 1)
    rs_step(0, 1, 0)
    rs_step(1, 2, 0)
    rs_step(1, 2, 1)
    returned(1)
    rs_step(0, 2, 1)
    rs_step(1, 3, 0)
    rs_step(0, 2, 0)
    rs_step(1, 3, 1)
    returned(0)
    rs_step(0, 3, 1)
    rs_step(0, 3, 0)

    for d in range(1, NDP):
        tgcopy(d, lax.rem(dp - d + NDP, NDP)).wait_recv()
    store(2, tg_ref, tg_out)
    for o in range(1, NZ):
        losscopy(o).wait_recv()
    losses = losss[0]
    for o in range(1, NZ):
        losses = losses + lossr[o]
    loss_ref[...] = losses[0:3]
    store(3, loss_ref, loss_out)
    for chunk in (0, 1):
        rs(1, 3, chunk).wait_recv()
    for chunk in (1, 0):
        rs(0, 3, chunk).wait_recv()
    qg_ref[...] = part[0, 0:QD, :] + rsR[0, 3].astype(F32) + rsR[1, 3].astype(F32)
    store(4, qg_ref, qg_out)
    finish()


def place_outputs(*refs):
    for source, target in zip(refs[0:5], refs[5:10]):
        target[...] = source[...]


def per_device(queries, shortlist, slab_slot, top_target, leaf_target, top_weight, mid_weight, leaf_weight):
    hbm = pl.BlockSpec(memory_space=pltpu.HBM)
    vmem = pl.BlockSpec(memory_space=pltpu.VMEM)
    sem = pltpu.SemaphoreType.DMA
    results = (
        jax.ShapeDtypeStruct((QD, D), F32),
        jax.ShapeDtypeStruct((64, D), F32),
        jax.ShapeDtypeStruct((2, D), F32),
        jax.ShapeDtypeStruct((2, LEAF, D), F32),
        jax.ShapeDtypeStruct((3, QD), F32),
    )
    scratch = [
        pltpu.VMEM((NZ, QD, D), BF16),
        pltpu.VMEM((SHORT, QD), jnp.int32),
        pltpu.VMEM((1, BLOCKS), jnp.int32),
        pltpu.VMEM((1, QD), jnp.int32),
        pltpu.VMEM((1, QD), jnp.int32),
        pltpu.VMEM((2, D), BF16),
        pltpu.VMEM((NZ, 8, 128), F32),
        pltpu.VMEM((NZ, 8, 128), F32),
        pltpu.VMEM((NX, 64, D), BF16),
        pltpu.VMEM((272, D), BF16),
        pltpu.VMEM((STEPS, SLOTS, SLOTS), BF16),
        pltpu.VMEM((8, SLOTS), jnp.int32),
        pltpu.VMEM((STEPS, PLANE, ROWS, D), BF16),
        pltpu.VMEM((STEPS, PLANE, ROWS, D), BF16),
        pltpu.VMEM((STEPS, LEAF + 8, SLOTS), F32),
        pltpu.VMEM((STEPS, 256, SLOTS), F32),
        pltpu.VMEM((GROUPS, 8, 128), F32),
        pltpu.VMEM((PLANE, 8, 128), F32),
        pltpu.VMEM((GROUPS, 8, 128), F32),
        pltpu.VMEM((PLANE, 8, 128), F32),
        pltpu.VMEM((GROUPS, 8, 128), F32),
        pltpu.VMEM((PLANE, 8, 128), F32),
        pltpu.VMEM((GROUPS, 8, 128), F32),
        pltpu.VMEM((PLANE, 8, 128), F32),
        pltpu.VMEM((2, NZ, 128), F32),
        pltpu.VMEM((NZ, 2, NZ, 128), F32),
        pltpu.VMEM((3, NZ, 128), F32),
        pltpu.VMEM((NZ, 128), F32),
        pltpu.VMEM((NZ, NZ, 128), F32),
        pltpu.VMEM((STEPS, SLOTS, D), F32),
        pltpu.VMEM((STEPS, PLANE, ROWS, D), BF16),
        pltpu.VMEM((STEPS, PLANE, ROWS, D), BF16),
        pltpu.VMEM((2, PLANE // 2, 8, D), F32),
        pltpu.VMEM((PLANE // 2, 8, D), F32),
        pltpu.VMEM((PLANE // 2, 8, D), F32),
        pltpu.VMEM((PLANE // 2, 8, D), F32),
        pltpu.VMEM((NZ, 8, 128), F32),
        pltpu.VMEM((NZ, 8, 128), F32),
        pltpu.VMEM((2, 4, QD, D), BF16),
        pltpu.VMEM((2, 4, QD, D), BF16),
        *[pltpu.VMEM(result.shape, F32) for result in results],
        sem((13,)), sem((13,)),
        sem((2, 4, 4)), sem((2, 4, 4)),
        sem((2, 4, 2)), sem((2, 4, 2)),
        sem((4, NZ)), sem((4, NZ)),
        sem((NX,)), sem((NX,)),
        sem((NDP,)), sem((NDP,)),
        sem((9,)), sem((5,)),
    ]
    arrays = pl.pallas_call(
        kernel,
        out_shape=results,
        in_specs=[hbm] * 8,
        out_specs=(hbm,) * 5,
        scratch_shapes=scratch,
        compiler_params=pltpu.CompilerParams(
            collective_id=0, has_side_effects=True, vmem_limit_bytes=60 << 20
        ),
    )(
        queries, shortlist.T, slab_slot.reshape(1, -1), top_target.reshape(1, -1), leaf_target.reshape(1, -1),
        leaf_weight, mid_weight, top_weight,
    )
    return pl.pallas_call(
        place_outputs,
        out_shape=results,
        in_specs=[vmem] * 5,
        out_specs=(vmem,) * 5,
        compiler_params=pltpu.CompilerParams(vmem_limit_bytes=60 << 20),
    )(*arrays)


def solution(mesh):
    both = ("dp", "label")
    in_specs = (
        P(both, None), P(both, None), P(), P(both), P(both),
        P("label", None), P(both, None), P(both, None, None),
    )
    out_specs = (
        P(both, None), P("label", None), P(both, None), P(both, None, None), P(None, both),
    )
    return jax.shard_map(
        per_device, mesh=mesh, in_specs=in_specs, out_specs=out_specs, check_vma=False
    )
```
